128 devices in a mesh: view: 8 (over y, core), space: 16 (over z, x).
Axes of the slice: x: 4, y: 4, z: 4, core: 2. Of those that a mesh axis runs over, the one named last changes fastest.
Arguments:
- brick_feats: bfloat16 [8192, 512, 32], P(('view', 'space')), may hold values from -6 to 6
- interp_weights: bfloat16 [16384, 128, 512], P(('view', 'space')), may hold values from 0 to 0.099609375
- block_owner: int32 [16384, 1], P(('view', 'space')), may hold values from 0 to 127; in each aligned block of 128 rows (0 to 127, 128 to 255, ...) at most 2 rows name the same one
- block_brick: int32 [16384, 1], P(('view', 'space')), may hold values from 0 to 63
- sample_count: int32 [65536], P(('view', 'space')), may hold values from 1 to 32
- target: float32 [3, 65536], P(None, ('view', 'space')), may hold values from 0 to 1
- w_in: bfloat16 [32, 256], replicated, may hold values from -1 to 1
- b_in: float32 [256], replicated, may hold values from -3 to 3
- w_hid: bfloat16 [256, 256], replicated, may hold values from -0.5 to 0.5
- b_hid: float32 [256], replicated, may hold values from -3 to 3
- w_out: bfloat16 [4, 256], replicated, may hold values from -0.5 to 0.5
- b_out: float32 [4], replicated, may hold values from -2 to 2
Outputs:
- brick_grad: float32 [8192, 512, 32], P(('view', 'space'))
- color: float32 [3, 65536], P(None, ('view', 'space'))
- g_w_in: float32 [32, 256], replicated
- g_b_in: float32 [256], replicated
- g_w_hid: float32 [256, 256], replicated
- g_b_hid: float32 [256], replicated
- g_w_out: float32 [4, 256], replicated
- g_b_out: float32 [4], replicated
The draws below stay inside these ranges and needn't reach their ends.
Inputs may be any that keep to these rules, and one draw needn't show every extreme that they name: `block_owner`: among the 128 rows of one device no owner appears more than 2 times, and some owner appears exactly 2 times in some devices' rows.
All inputs are finite; a program needn't handle non-finite values.
Results may differ from the reference program's by a relative error of at most 0.0065.
The reference program's roundings to bfloat16 on the way (of `feats`, `act_one`, `act_two`, `d_raw_b`, `d_two_b`, `d_one_b` and `d_feats`) count: a program that leaves them out, or rounds other values in their place, can miss the bound.
Values may be sent and summed in bfloat16 or wider, within the bound.
No kernel may reach another device: no remote copies, remote signals or barrier semaphores. Data moves between devices by JAX's collectives and lax.ppermute only.
A program may use at most 256 MiB of HBM per device.

```python
import math
import jax
import jax.numpy as jnp
import numpy as np
from jax import lax

FEAT = 32
VOX = 512
WIDTH = 256
BLOCK = 128
RAY_LEN = 32
SB = 128
BRK_DEV = 64
CAP = 2
BLOCKS = 16384
BRICKS = 8192
RAYS = 65536
DEVICES = 128


def touch_ends(values, rng, least, largest):
    index_at = [jax.random.randint(jax.random.fold_in(rng, axis), (), 0, length) for axis, length in enumerate(values.shape)]
    widest = values.shape.index(max(values.shape))
    neighbour = index_at[:widest] + [(index_at[widest] + 1) % values.shape[widest]] + index_at[widest + 1:]
    return values.at[tuple(index_at)].set(least).at[tuple(neighbour)].set(largest)


def level_of(key, dims, shards, least, largest):
    gain, own = 1.0, jax.random.fold_in(key, 6)
    for axis_at, blocks in shards:
        draws = jnp.exp(jax.random.uniform(jax.random.fold_in(own, axis_at), (blocks,), jnp.float32, least / len(shards), largest / len(shards)))
        gain = gain * jnp.repeat(draws, dims[axis_at] // blocks).reshape([-1 if axis == axis_at else 1 for axis in range(len(dims))])
    return gain


def shared_out(key, own, number, rows, amount, top, bound, skew):
    ranking = jax.random.permutation(key, amount)
    packed, usual = portions_of(amount, rows * top, bound, skew, True), portions_of(amount, rows * top, bound, skew, False)
    places = jnp.arange(amount)

    def named(tallies, offset_by):
        used = int((tallies > 0).sum())
        fixed = max(1, used // 4)
        moved = fixed + (places - fixed + offset_by * (used - fixed)) % max(1, amount - fixed)
        return jnp.zeros((amount,), jnp.int32).at[ranking[jnp.where(places < fixed, places, moved)]].set(jnp.asarray(tallies, jnp.int32))

    tallies = jnp.where(number % 4 == 0, named(packed, number // 4), named(usual, number - number // 4 - 1))
    mixed = jax.random.permutation(jax.random.fold_in(own, 3), amount)
    giver, receiver = mixed[0:amount // 2 * 2:2], mixed[1:amount // 2 * 2:2]
    margin = jnp.minimum(tallies[giver] - 1, bound - tallies[receiver]) // 2
    margin = jnp.where((giver == ranking[0]) | (receiver == ranking[0]) | (tallies[receiver] == 0), 0, jnp.maximum(margin, 0))
    moved = jax.random.randint(jax.random.fold_in(own, 4), (amount // 2,), 0, 1 << 20) % (margin + 1)
    tallies = tallies.at[giver].add(-moved).at[receiver].add(moved)
    labels = jnp.searchsorted(jnp.cumsum(tallies), jnp.arange(rows * top), side="right").astype(jnp.int32)
    listing = labels.reshape(top, rows).T
    listing = listing[jax.random.permutation(jax.random.fold_in(own, 1), rows)]
    offset_by = jax.random.randint(jax.random.fold_in(own, 2), (rows, 1), 0, top)
    return jnp.take_along_axis(listing, (jnp.arange(top)[None, :] + offset_by) % top, axis=1)


def portions_of(amount, total, limit, slope, full):
    weights = [(1 << 20) // math.isqrt(standing ** slope) + 1 for standing in range(1, amount + 1)]
    largest = limit if full else min(limit, max(-(-total // amount), total * weights[0] // sum(weights)))
    least = 1 if total - largest >= amount - 1 else 0
    given, rest = [largest] + [least] * (amount - 1), total - largest - least * (amount - 1)
    while rest > 0:
        movable = [i for i in range(1, amount) if given[i] < largest] or [i for i in range(1, amount) if given[i] < limit]
        whole, budget = sum([weights[i] for i in movable]), rest
        for i in movable:
            extra = min(limit - given[i], max(1, budget * weights[i] // whole), rest)
            given[i] = given[i] + extra
            rest = rest - extra
    return np.array(given)


def scatter_about(stream_key, extent, scale, most, shards=(), dtype=jnp.bfloat16):
    loudness = level_of(stream_key, extent, shards, -0.22, 0.18) if shards else 1.0
    result = jax.random.normal(stream_key, extent, jnp.float32) * scale * loudness
    return jnp.minimum(jnp.maximum(result, -most), most).astype(dtype)


def setup_inputs(seed: int = 0) -> dict:
    splits = jax.random.split(jax.random.key(seed), 13)
    brick_feats = scatter_about(splits[0], (BRICKS, VOX, FEAT), 1.0, 6.0, ((0, 128),))
    interp_weights = jnp.clip(0.099609375 * jax.random.uniform(splits[1], (BLOCKS, BLOCK, VOX), jnp.float32) ** level_of(splits[1], (BLOCKS, BLOCK, VOX), ((0, 128),), -0.2, 0.2), 0.0, 0.099609375).astype(jnp.bfloat16)
    block_owner_keys = jax.random.split(jax.random.fold_in(splits[2], 1), BLOCKS // SB)
    block_owner_turns = jax.random.permutation(jax.random.fold_in(splits[2], 3), BLOCKS // SB)
    block_owner = jax.vmap(lambda own, number: shared_out(jax.random.fold_in(splits[2], 2), own, number, SB, DEVICES, 1, CAP, 2))(block_owner_keys, block_owner_turns).reshape((BLOCKS, 1))
    block_brick = touch_ends(jax.random.randint(splits[3], (BLOCKS, 1), 0, BRK_DEV), jax.random.fold_in(splits[3], 1), 0, BRK_DEV - 1).astype(jnp.int32)
    sample_count = touch_ends(jax.random.randint(splits[4], (RAYS,), 1, RAY_LEN + 1), jax.random.fold_in(splits[4], 1), 1, RAY_LEN).astype(jnp.int32)
    target = jnp.clip(1.0 * jax.random.uniform(splits[5], (3, RAYS), jnp.float32) ** level_of(splits[5], (3, RAYS), ((1, 128),), -0.2, 0.2), 0.0, 1.0)
    w_in = scatter_about(splits[6], (FEAT, WIDTH), FEAT ** -0.5, 1.0)
    b_in = scatter_about(splits[7], (WIDTH,), 0.5, 3.0, (), jnp.float32)
    w_hid = scatter_about(splits[8], (WIDTH, WIDTH), (WIDTH // 2) ** -0.5, 0.5)
    b_hid = scatter_about(splits[9], (WIDTH,), 0.5, 3.0, (), jnp.float32)
    w_out = scatter_about(splits[10], (4, WIDTH), (WIDTH // 2) ** -0.5, 0.5)
    b_out = scatter_about(splits[11], (4,), 0.5, 2.0, (), jnp.float32)
    return dict(brick_feats=brick_feats, interp_weights=interp_weights, block_owner=block_owner, block_brick=block_brick, sample_count=sample_count, target=target, w_in=w_in, b_in=b_in, w_hid=w_hid, b_hid=b_hid, w_out=w_out, b_out=b_out)


step_len = 0.05

def contract_rows(left, right):
    return lax.dot_general(left, right, (((0,), (0,)), ((), ())), preferred_element_type=jnp.float32)

def contract_cols(left, right):
    return lax.dot_general(left, right, (((1,), (1,)), ((), ())), preferred_element_type=jnp.float32)

def composite(raw_out, counts, goal_rgb):
    ray_count = counts.shape[0]
    shaped = raw_out.reshape(ray_count, RAY_LEN, 4)
    sigma = jax.nn.softplus(shaped[:, :, 0])
    shades = jax.nn.sigmoid(shaped[:, :, 1:])
    places = lax.broadcasted_iota(jnp.int32, (ray_count, RAY_LEN), 1)
    is_live = (places < counts[:, None]).astype(jnp.float32)
    depth = step_len * sigma * is_live
    alpha = 1.0 - jnp.exp(-depth)
    trans = jnp.exp(depth - jnp.cumsum(depth, axis=1))
    weight = trans * alpha
    rendered = lax.optimization_barrier(jnp.sum(weight[:, :, None] * shades, axis=1)).T
    loss = 0.5 * jnp.sum(jnp.square(rendered - goal_rgb))
    return (loss, rendered)

def network_pass(feats, counts, goal_rgb, w_in, b_in, w_hid, b_hid, w_out, b_out):
    pre_one = jnp.dot(feats, w_in, preferred_element_type=jnp.float32) + b_in
    act_one = jnp.maximum(pre_one, 0.0).astype(jnp.bfloat16)
    pre_two = jnp.dot(act_one, w_hid, preferred_element_type=jnp.float32) + b_hid
    act_two = jnp.maximum(pre_two, 0.0).astype(jnp.bfloat16)
    raw_out = contract_cols(act_two, w_out) + b_out

    def render_loss(values):
        return composite(values, counts, goal_rgb)
    loss, pullback, rendered = jax.vjp(render_loss, raw_out, has_aux=True)
    d_raw = pullback(jnp.ones((), jnp.float32))[0]
    d_raw_b = d_raw.astype(jnp.bfloat16)
    g_w_out = contract_rows(d_raw_b, act_two)
    g_b_out = lax.optimization_barrier(jnp.sum(d_raw, axis=0))
    d_two = jnp.dot(d_raw_b, w_out, preferred_element_type=jnp.float32) * (pre_two > 0.0)
    d_two_b = d_two.astype(jnp.bfloat16)
    g_w_hid = contract_rows(act_one, d_two_b)
    g_b_hid = lax.optimization_barrier(jnp.sum(d_two, axis=0))
    d_one = contract_cols(d_two_b, w_hid) * (pre_one > 0.0)
    d_one_b = d_one.astype(jnp.bfloat16)
    g_w_in = contract_rows(feats, d_one_b)
    g_b_in = lax.optimization_barrier(jnp.sum(d_one, axis=0))
    d_feats = contract_cols(d_one_b, w_in).astype(jnp.bfloat16)
    return (rendered, d_feats, (g_w_in, g_b_in, g_w_hid, g_b_hid, g_w_out, g_b_out))

def reference(brick_feats, interp_weights, block_owner, block_brick, sample_count, target, w_in, b_in, w_hid, b_hid, w_out, b_out):
    brick_ids = (block_owner[:, 0] * BRK_DEV + block_brick[:, 0]).astype(jnp.int32)
    per_dev = SB * BLOCK // RAY_LEN
    weights_grouped = interp_weights.reshape(DEVICES, SB, BLOCK, VOX)
    ids_grouped = brick_ids.reshape(DEVICES, SB)
    counts_grouped = sample_count.reshape(DEVICES, per_dev)
    target_grouped = target.reshape(3, DEVICES, per_dev).transpose(1, 0, 2)

    def one_group(state_now, inputs):
        brick_grads, sums_now = state_now
        weights, group_ids, counts, goal_rgb = inputs
        bricks = brick_feats[group_ids]
        feats = jnp.einsum('bsv,bvf->bsf', weights.astype(jnp.float32), bricks.astype(jnp.float32))
        feats = feats.astype(jnp.bfloat16).reshape(SB * BLOCK, FEAT)
        rendered, d_feats, param_sums = network_pass(feats, counts, goal_rgb, w_in, b_in, w_hid, b_hid, w_out, b_out)
        block_grad = jnp.einsum('bsv,bsf->bvf', weights.astype(jnp.float32), d_feats.reshape(SB, BLOCK, FEAT).astype(jnp.float32))
        brick_grads = brick_grads.at[group_ids].add(block_grad)
        sums_now = tuple((first + second for first, second in zip(sums_now, param_sums)))
        return ((brick_grads, sums_now), rendered)
    start_sums = (jnp.zeros((FEAT, WIDTH), jnp.float32), jnp.zeros((WIDTH,), jnp.float32), jnp.zeros((WIDTH, WIDTH), jnp.float32), jnp.zeros((WIDTH,), jnp.float32), jnp.zeros((4, WIDTH), jnp.float32), jnp.zeros((4,), jnp.float32))
    start_state = (jnp.zeros((BRICKS, VOX, FEAT), jnp.float32), start_sums)
    final_state, colors = lax.scan(one_group, start_state, (weights_grouped, ids_grouped, counts_grouped, target_grouped))
    brick_grad, totals = final_state
    color = colors.transpose(1, 0, 2).reshape(3, RAYS)
    scaled = tuple((total / RAYS for total in totals))
    return (brick_grad, color, scaled[0], scaled[1], scaled[2], scaled[3], scaled[4], scaled[5])
```

```python
import functools

import jax
import jax.numpy as jnp
from jax import lax
from jax.experimental import pallas as pl
from jax.experimental.pallas import tpu as pltpu
from jax.sharding import PartitionSpec as P

FEAT = 32
VOX = 512
WIDTH = 256
BLOCK = 128
RAY_LEN = 32
GROUP = 8
GRAD_ROWS = 1024

AXES = ("view", "space")
step_len = 0.05
F32 = jnp.float32
BF16 = jnp.bfloat16


def dot_nn(left, right, precision=None):
    return lax.dot_general(
        left, right, (((1,), (0,)), ((), ())), precision=precision, preferred_element_type=F32
    )


def dot_nt(left, right, precision=None):
    return lax.dot_general(
        left, right, (((1,), (1,)), ((), ())), precision=precision, preferred_element_type=F32
    )


def lane_sums(values, matrix):
    return dot_nn(values, matrix, precision=lax.Precision.HIGHEST)


def render_grad(raw, live, goal, before, within, after):
    rows = live.shape[0]
    small = jnp.exp(-jnp.abs(raw[0]))
    sigma = jnp.maximum(raw[0], 0.0) + jnp.log1p(small)
    slope = jnp.where(raw[0] >= 0.0, 1.0, small) / (1.0 + small)
    shades = [jax.nn.sigmoid(channel) for channel in raw[1:]]
    depth = step_len * sigma * live
    faded = jnp.exp(-depth)
    trans = jnp.exp(depth - lane_sums(depth, before))
    weight = trans * (1.0 - faded)
    stacked = jnp.concatenate([weight * shade for shade in shades], axis=0)
    color = lane_sums(stacked, within)
    colors = [color[c * rows : (c + 1) * rows] for c in range(3)]
    miss = [colors[c] - goal[c] for c in range(3)]
    d_weight = miss[0] * shades[0] + miss[1] * shades[1] + miss[2] * shades[2]
    d_depth = d_weight * (trans * faded) - lane_sums(d_weight * weight, after)
    d_raw = [step_len * live * d_depth * slope]
    for c in range(3):
        d_raw.append(weight * miss[c] * shades[c] * (1.0 - shades[c]))
    return colors, d_raw


def lane_matrices():
    row = lax.broadcasted_iota(jnp.int32, (BLOCK, BLOCK), 0)
    col = lax.broadcasted_iota(jnp.int32, (BLOCK, BLOCK), 1)
    same = (row // RAY_LEN) == (col // RAY_LEN)
    before = (same & (row <= col)).astype(F32)
    after = (same & (row > col)).astype(F32)
    return before, same.astype(F32), after


def step_kernel(
    first,
    count_ref,
    block_ref,
    slot_ref,
    weights_hbm,
    bricks_hbm,
    samples_ref,
    goal_ref,
    w_in_ref,
    w_in_t_ref,
    b_in_ref,
    w_hid_ref,
    w_hid_t_ref,
    b_hid_ref,
    w_out_ref,
    w_out_t_ref,
    b_out_ref,
    lanes_ref,
    carried_ref,
    _,
    grads_hbm,
    color_ref,
    sums_ref,
    weights_buf,
    bricks_buf,
    grads_buf,
    raw_buf,
    d_raw_buf,
    live_buf,
    goal_buf,
    acc_hid,
    acc_in,
    acc_out,
    acc_b_hid,
    acc_b_in,
    acc_b_out,
    weights_sem,
    bricks_sem,
    grads_sem,
):
    total = count_ref[0]
    steps = (total + GROUP - 1) // GROUP
    width = GROUP * BLOCK

    def fetch(step, side):
        for k in range(GROUP):
            at = step * GROUP + k
            pltpu.make_async_copy(
                weights_hbm.at[block_ref[at]], weights_buf.at[side, k], weights_sem.at[side, k]
            ).start()
            pltpu.make_async_copy(
                bricks_hbm.at[slot_ref[at]], bricks_buf.at[side, k], bricks_sem.at[side, k]
            ).start()

    def arrive(side):
        for k in range(GROUP):
            pltpu.make_async_copy(
                weights_hbm.at[0], weights_buf.at[side, k], weights_sem.at[side, k]
            ).wait()
            pltpu.make_async_copy(
                bricks_hbm.at[0], bricks_buf.at[side, k], bricks_sem.at[side, k]
            ).wait()

    def send(step, side):
        for k in range(GROUP):
            at = step * GROUP + k

            @pl.when(at < total)
            def _():
                pltpu.make_async_copy(
                    grads_buf.at[side, k],
                    grads_hbm.at[slot_ref[at], 0 if first else 1],
                    grads_sem.at[side, k],
                ).start()

    def settle(step, side):
        for k in range(GROUP):
            at = step * GROUP + k

            @pl.when((step >= 0) & (at < total))
            def _():
                pltpu.make_async_copy(
                    grads_buf.at[side, k], grads_hbm.at[0, 0], grads_sem.at[side, k]
                ).wait()

    @pl.when(steps > 0)
    def _():
        fetch(0, 0)

    for ref in (acc_hid, acc_in, acc_out, acc_b_hid, acc_b_in, acc_b_out, color_ref):
        ref[...] = jnp.zeros_like(ref)

    def one_step(step, state):
        side = step % 2
        arrive(side)

        @pl.when(step + 1 < steps)
        def _():
            fetch(step + 1, 1 - side)

        for k in range(GROUP):
            at = step * GROUP + k
            block = block_ref[at]
            used = jnp.where(at < total, samples_ref[pl.ds(block, 1), :], 0)
            live_buf[pl.ds(k, 1), :] = used
            for c in range(3):
                goal_buf[c, pl.ds(k, 1), :] = goal_ref[c, pl.ds(block, 1), :]
        place = lax.broadcasted_iota(jnp.int32, (GROUP, BLOCK), 1) % RAY_LEN
        live = (place < live_buf[...]).astype(F32)

        feats = jnp.concatenate(
            [dot_nt(bricks_buf[side, k], weights_buf[side, k]) for k in range(GROUP)], axis=1
        ).astype(BF16)
        pre_one = dot_nn(w_in_t_ref[...], feats) + b_in_ref[...]
        act_one = jnp.maximum(pre_one, 0.0).astype(BF16)
        pre_two = dot_nn(w_hid_t_ref[...], act_one) + b_hid_ref[...]
        act_two = jnp.maximum(pre_two, 0.0).astype(BF16)
        raw = dot_nn(w_out_ref[...], act_two) + b_out_ref[...]
        for k in range(GROUP):
            for c in range(4):
                raw_buf[c, k : k + 1, :] = raw[c : c + 1, k * BLOCK : (k + 1) * BLOCK]
        colors, d_raw = render_grad(
            [raw_buf[c] for c in range(4)],
            live,
            [goal_buf[c] for c in range(3)],
            lanes_ref[0],
            lanes_ref[1],
            lanes_ref[2],
        )
        for k in range(GROUP):
            at = step * GROUP + k
            row = jnp.where(at < total, block_ref[at], BLOCK)
            for c in range(3):
                color_ref[c, pl.ds(row, 1), :] = colors[c][k : k + 1]
            for c in range(4):
                d_raw_buf[c : c + 1, k * BLOCK : (k + 1) * BLOCK] = d_raw[c][k : k + 1]
        for c in range(4):
            acc_b_out[c] += d_raw[c]
        d_raw_b = d_raw_buf[...].astype(BF16)
        acc_out[...] += dot_nt(d_raw_b, act_two)
        d_two = jnp.where(pre_two > 0.0, dot_nn(w_out_t_ref[...], d_raw_b), 0.0)
        d_two_b = d_two.astype(BF16)
        acc_hid[...] += dot_nt(act_one, d_two_b)
        d_one = jnp.where(pre_one > 0.0, dot_nn(w_hid_ref[...], d_two_b), 0.0)
        d_one_b = d_one.astype(BF16)
        acc_in[...] += dot_nt(feats, d_one_b)
        b_two = acc_b_hid[...]
        b_one = acc_b_in[...]
        for k in range(GROUP):
            b_two += d_two[:, k * BLOCK : (k + 1) * BLOCK]
            b_one += d_one[:, k * BLOCK : (k + 1) * BLOCK]
        acc_b_hid[...] = b_two
        acc_b_in[...] = b_one
        d_feats = dot_nn(w_in_ref[...], d_one_b).astype(BF16)
        settle(step - 2, side)
        for k in range(GROUP):
            grads_buf[side, k] = dot_nn(
                d_feats[:, k * BLOCK : (k + 1) * BLOCK], weights_buf[side, k]
            ).astype(BF16)
        send(step, side)
        return state

    lax.fori_loop(0, steps, one_step, 0)

    settle(steps - 2, steps % 2)
    settle(steps - 1, (steps + 1) % 2)

    ones = jnp.ones((8, BLOCK), F32)

    def over_lanes(values):
        return dot_nt(ones, values, precision=lax.Precision.HIGHEST)

    half = WIDTH // 2
    sums_ref[0:256, :] = acc_hid[:, :half]
    sums_ref[256:512, :] = acc_hid[:, half:]
    sums_ref[512:544, :] = acc_in[:, :half]
    sums_ref[544:576, :] = acc_in[:, half:]
    sums_ref[576:584, :] = acc_out[:, :half]
    sums_ref[584:592, :] = acc_out[:, half:]
    b_hid_row = over_lanes(acc_b_hid[...])
    b_in_row = over_lanes(acc_b_in[...])
    sums_ref[592:600, :] = b_hid_row[:, :half]
    sums_ref[600:608, :] = b_hid_row[:, half:]
    sums_ref[608:616, :] = b_in_row[:, :half]
    sums_ref[616:624, :] = b_in_row[:, half:]
    sums_ref[624:632, :] = jnp.zeros((8, BLOCK), F32)
    for c in range(4):
        sums_ref[624 + c : 625 + c, :] = jnp.sum(acc_b_out[c], axis=0, keepdims=True)
    sums_ref[632:GRAD_ROWS, :] = jnp.zeros((GRAD_ROWS - 632, BLOCK), F32)
    if not first:
        sums_ref[...] += carried_ref[...]


def run_blocks(first, total, blocks, slots, weights, bricks, samples, goal, params, carried, grads):
    vmem = pl.BlockSpec(memory_space=pltpu.VMEM)
    smem = pl.BlockSpec(memory_space=pltpu.SMEM)
    hbm = pl.BlockSpec(memory_space=pltpu.MemorySpace.HBM)
    amount = blocks.shape[0] if first else blocks.shape[0] // 8
    cost = pl.CostEstimate(
        flops=amount * 70_000_000, bytes_accessed=amount * 200_000, transcendentals=amount * 1000
    )
    return pl.pallas_call(
        functools.partial(step_kernel, first),
        out_shape=(
            jax.ShapeDtypeStruct((bricks.shape[0], 2, FEAT, VOX), BF16),
            jax.ShapeDtypeStruct((3, BLOCK + 8, BLOCK), F32),
            jax.ShapeDtypeStruct((GRAD_ROWS, BLOCK), F32),
        ),
        in_specs=[smem, smem, smem, hbm, hbm] + [vmem] * 13 + [hbm],
        out_specs=(hbm, vmem, vmem),
        scratch_shapes=[
            pltpu.VMEM((2, GROUP, BLOCK, VOX), BF16),
            pltpu.VMEM((2, GROUP, FEAT, VOX), BF16),
            pltpu.VMEM((2, GROUP, FEAT, VOX), BF16),
            pltpu.VMEM((4, GROUP, BLOCK), F32),
            pltpu.VMEM((8, GROUP * BLOCK), F32),
            pltpu.VMEM((GROUP, BLOCK), jnp.int32),
            pltpu.VMEM((3, GROUP, BLOCK), F32),
            pltpu.VMEM((WIDTH, WIDTH), F32),
            pltpu.VMEM((FEAT, WIDTH), F32),
            pltpu.VMEM((8, WIDTH), F32),
            pltpu.VMEM((WIDTH, BLOCK), F32),
            pltpu.VMEM((WIDTH, BLOCK), F32),
            pltpu.VMEM((4, GROUP, BLOCK), F32),
            pltpu.SemaphoreType.DMA((2, GROUP)),
            pltpu.SemaphoreType.DMA((2, GROUP)),
            pltpu.SemaphoreType.DMA((2, GROUP)),
        ],
        compiler_params=pltpu.CompilerParams(vmem_limit_bytes=60 << 20),
        input_output_aliases={} if first else {18: 0},
        cost_estimate=cost,
        name="blocks_first" if first else "blocks_second",
    )(total, blocks, slots, weights, bricks, samples, goal, *params, carried, grads)


TAKE = 8


def collect_kernel(ids_ref, grads_ref, out_ref):
    step = pl.program_id(0)

    @pl.when(step == 0)
    def _():
        out_ref[...] = jnp.zeros_like(out_ref)

    for k in range(TAKE):
        for r in range(2):
            brick = ids_ref[2 * (step * TAKE + k) + r]

            @pl.when(brick >= 0)
            def _():
                out_ref[brick] += grads_ref[k, r].astype(F32)


def collect(ids, grads, own):
    amount = grads.shape[0]
    return pl.pallas_call(
        collect_kernel,
        out_shape=jax.ShapeDtypeStruct((own, FEAT, VOX), F32),
        grid_spec=pltpu.PrefetchScalarGridSpec(
            num_scalar_prefetch=1,
            grid=(amount // TAKE,),
            in_specs=[pl.BlockSpec((TAKE, 2, FEAT, VOX), lambda i, ids: (i, 0, 0, 0))],
            out_specs=pl.BlockSpec((own, FEAT, VOX), lambda i, ids: (0, 0, 0)),
        ),
        compiler_params=pltpu.CompilerParams(vmem_limit_bytes=60 << 20),
        cost_estimate=pl.CostEstimate(
            flops=amount * FEAT * VOX, bytes_accessed=amount * FEAT * VOX * 2, transcendentals=0
        ),
        name="collect",
    )(ids, grads)


def exchange(values):
    return lax.all_to_all(values, AXES, split_axis=0, concat_axis=0, tiled=True)


def scatter_sum(parts, axis):
    size = parts.shape[0]
    me = lax.axis_index(axis)
    pieces = [lax.dynamic_index_in_dim(parts, me, keepdims=False)]
    for shift in range(1, size):
        piece = lax.dynamic_index_in_dim(parts, (me + shift) % size, keepdims=False)
        pieces.append(lax.ppermute(piece, axis, [(i, (i + shift) % size) for i in range(size)]))
    return functools.reduce(jnp.add, pieces)


def gather_all(part, axis, size):
    me = lax.axis_index(axis)
    pieces = [part]
    for shift in range(1, size):
        pieces.append(lax.ppermute(part, axis, [((i + shift) % size, i) for i in range(size)]))
    twice = jnp.concatenate(pieces + pieces)
    rows = part.shape[0]
    return lax.dynamic_slice_in_dim(twice, (size - me) % size * rows, size * rows)


def sum_over_devices(sums):
    space, view = lax.axis_size("space"), lax.axis_size("view")
    part = scatter_sum(sums.reshape(space, GRAD_ROWS // space, BLOCK), "space")
    part = scatter_sum(part.reshape(view, GRAD_ROWS // (space * view), BLOCK), "view")
    return gather_all(gather_all(part, "view", view), "space", space)


def network_params(w_in, b_in, w_hid, b_hid, w_out, b_out):
    w_out_rows = jnp.pad(w_out, ((0, 4), (0, 0)))
    return (
        w_in,
        w_in.T,
        b_in[:, None],
        w_hid,
        w_hid.T,
        b_hid[:, None],
        w_out_rows,
        w_out_rows.T,
        jnp.pad(b_out, (0, 4))[:, None],
        jnp.stack(lane_matrices()),
    )


def body(
    brick_feats,
    interp_weights,
    block_owner,
    block_brick,
    sample_count,
    target,
    w_in,
    b_in,
    w_hid,
    b_hid,
    w_out,
    b_out,
):
    own_blocks = interp_weights.shape[0]
    own_bricks = brick_feats.shape[0]
    dev_count = lax.axis_size(AXES)
    owners = block_owner[:, 0]
    local_ids = block_brick[:, 0]
    row_index = lax.broadcasted_iota(jnp.int32, (own_blocks, own_blocks), 0)
    col_index = lax.broadcasted_iota(jnp.int32, (own_blocks, own_blocks), 1)
    same = owners[:, None] == owners[None, :]
    ranks = jnp.sum((same & (col_index < row_index)).astype(jnp.int32), axis=1)
    ranks_c = jnp.sum((same & (row_index < col_index)).astype(jnp.int32), axis=0)

    owner_row = row_index == owners[None, :]
    wish = [
        jnp.max(jnp.where(owner_row & (ranks_c == r)[None, :], local_ids[None, :], -1), axis=1)
        for r in range(2)
    ]
    asked = exchange(jnp.stack(wish, axis=1).reshape(dev_count, 1, 2)).reshape(dev_count, 2)

    lists = []
    for r in range(2):
        mine = ranks == r
        place = jnp.sum(((col_index < row_index) & (ranks_c == r)[None, :]).astype(jnp.int32), axis=1)
        total = jnp.sum(mine.astype(jnp.int32))
        hit = (place[:, None] == col_index) & mine[:, None]
        blocks = jnp.sum(jnp.where(hit, row_index, 0), axis=0)
        slots = jnp.sum(jnp.where(hit, owners[:, None], 0), axis=0)
        last = jnp.max(jnp.where(mine, row_index[:, 0], 0))
        last_slot = jnp.sum(jnp.where(mine & (row_index[:, 0] == last), owners, 0))
        empty = col_index[0] >= total
        blocks = jnp.where(empty, last, blocks)
        slots = jnp.where(empty, last_slot, slots)
        lists.append((total[None], blocks, slots))

    bricks_t = jnp.swapaxes(brick_feats, 1, 2)
    fetched = [exchange(bricks_t[jnp.maximum(asked[:, r], 0)]) for r in range(2)]

    samples = jnp.repeat(sample_count, RAY_LEN).reshape(own_blocks, BLOCK)
    goal = jnp.repeat(target, RAY_LEN, axis=1).reshape(3, own_blocks, BLOCK)
    params = network_params(w_in, b_in, w_hid, b_hid, w_out, b_out)
    nothing = jnp.zeros((8, BLOCK), F32)
    grads, color_0, sums = run_blocks(
        True, *lists[0], interp_weights, fetched[0], samples, goal, params, nothing, nothing
    )
    grads, color_1, sums = run_blocks(
        False, *lists[1], interp_weights, fetched[1], samples, goal, params, sums, grads
    )
    brick_grad = collect(asked.reshape(-1), exchange(grads), own_bricks)
    brick_grad = jnp.swapaxes(brick_grad, 1, 2)

    totals = sum_over_devices(sums) / (sample_count.shape[0] * dev_count)
    half = WIDTH // 2

    def joined(start, rows):
        return jnp.concatenate([totals[start : start + rows], totals[start + rows : start + 2 * rows]], axis=1)

    g_w_hid = joined(0, WIDTH)
    g_w_in = joined(2 * WIDTH, FEAT)
    g_w_out = joined(576, 8)[:4]
    g_b_hid = joined(592, 8)[0]
    g_b_in = joined(608, 8)[0]
    g_b_out = jnp.sum(totals[624:628], axis=1)
    color = (color_0 + color_1)[:, :own_blocks, ::RAY_LEN].reshape(3, -1)
    return (brick_grad, color, g_w_in, g_b_in, g_w_hid, g_b_hid, g_w_out, g_b_out)


def solution(mesh):
    shared = P(AXES, None, None)
    return jax.shard_map(
        body,
        mesh=mesh,
        in_specs=(
            shared,
            shared,
            P(AXES, None),
            P(AXES, None),
            P(AXES),
            P(None, AXES),
            P(),
            P(),
            P(),
            P(),
            P(),
            P(),
        ),
        out_specs=(shared, P(None, AXES), P(), P(), P(), P(), P(), P()),
        check_vma=False,
    )
```

```python
import functools

import jax
import jax.numpy as jnp
from jax import lax
from jax.experimental import pallas as pl
from jax.experimental.pallas import tpu as pltpu
from jax.sharding import PartitionSpec as P

FEAT = 32
VOX = 512
WIDTH = 256
BLOCK = 128
RAY_LEN = 32
GROUP = 8
GRAD_ROWS = 1024

AXES = ("view", "space")
step_len = 0.05
F32 = jnp.float32
BF16 = jnp.bfloat16


def dot_nn(left, right, precision=None):
    return lax.dot_general(
        left, right, (((1,), (0,)), ((), ())), precision=precision, preferred_element_type=F32
    )


def dot_nt(left, right, precision=None):
    return lax.dot_general(
        left, right, (((1,), (1,)), ((), ())), precision=precision, preferred_element_type=F32
    )


def dot_tn(left, right):
    return lax.dot_general(
        left, right, (((0,), (0,)), ((), ())), preferred_element_type=F32
    )


def lane_sums(values, matrix):
    return dot_nn(values, matrix, precision=lax.Precision.HIGHEST)


def render_grad(raw, live, goal, before, within, after):
    rows = live.shape[0]
    small = jnp.exp(-jnp.abs(raw[0]))
    sigma = jnp.maximum(raw[0], 0.0) + jnp.log1p(small)
    slope = jnp.where(raw[0] >= 0.0, 1.0, small) / (1.0 + small)
    shades = [jax.nn.sigmoid(channel) for channel in raw[1:]]
    depth = step_len * sigma * live
    faded = jnp.exp(-depth)
    trans = jnp.exp(depth - lane_sums(depth, before))
    weight = trans * (1.0 - faded)
    stacked = jnp.concatenate([weight * shade for shade in shades], axis=0)
    color = lane_sums(stacked, within)
    colors = [color[c * rows : (c + 1) * rows] for c in range(3)]
    miss = [colors[c] - goal[c] for c in range(3)]
    d_weight = miss[0] * shades[0] + miss[1] * shades[1] + miss[2] * shades[2]
    d_depth = d_weight * (trans * faded) - lane_sums(d_weight * weight, after)
    d_raw = [step_len * live * d_depth * slope]
    for c in range(3):
        d_raw.append(weight * miss[c] * shades[c] * (1.0 - shades[c]))
    return colors, d_raw


def lane_matrices():
    row = lax.broadcasted_iota(jnp.int32, (BLOCK, BLOCK), 0)
    col = lax.broadcasted_iota(jnp.int32, (BLOCK, BLOCK), 1)
    same = (row // RAY_LEN) == (col // RAY_LEN)
    before = (same & (row <= col)).astype(F32)
    after = (same & (row > col)).astype(F32)
    return before, same.astype(F32), after


def plan_kernel(owner_ref, brick_ref, wish_ref, lists_ref):
    amount = owner_ref.shape[0]

    def clear(i, state):
        wish_ref[2 * i] = -1
        wish_ref[2 * i + 1] = -1
        return state

    lax.fori_loop(0, wish_ref.shape[0] // 2, clear, 0, unroll=8)

    def place(i, state):
        firsts, seconds = state
        owner = owner_ref[i]
        rank = jnp.where(wish_ref[2 * owner] >= 0, 1, 0)
        wish_ref[2 * owner + rank] = brick_ref[i]
        lists_ref[0, 1 + firsts] = i
        lists_ref[1, 1 + seconds] = i
        return firsts + 1 - rank, seconds + rank

    counts = lax.fori_loop(0, amount, place, (0, 0), unroll=4)
    for rank in range(2):
        lists_ref[rank, 0] = counts[rank]
        for k in range(GROUP):
            lists_ref[rank, 1 + counts[rank] + k] = 0


def plan(owners, bricks, dev_count):
    smem = pl.BlockSpec(memory_space=pltpu.SMEM)
    return pl.pallas_call(
        plan_kernel,
        out_shape=(
            jax.ShapeDtypeStruct((dev_count * 2,), jnp.int32),
            jax.ShapeDtypeStruct((2, owners.shape[0] + 2 * GROUP), jnp.int32),
        ),
        in_specs=[smem, smem],
        out_specs=(smem, smem),
        name="plan",
    )(owners, bricks)


def step_kernel(
    first,
    lists_ref,
    owner_ref,
    b_out_ref,
    weights_hbm,
    bricks_hbm,
    rays_ref,
    w_in_ref,
    b_in_ref,
    w_hid_ref,
    b_hid_ref,
    w_out_ref,
    carried_ref,
    _,
    grads_hbm,
    color_ref,
    sums_ref,
    weights_buf,
    bricks_buf,
    grads_buf,
    rays_buf,
    raw_buf,
    d_raw_buf,
    step_buf,
    lanes_buf,
    w_in_t,
    w_hid_t,
    w_out_rows,
    b_one_col,
    b_two_col,
    acc_hid,
    acc_in,
    acc_out,
    acc_b_hid,
    acc_b_in,
    acc_b_out,
    parts_buf,
    weights_sem,
    bricks_sem,
    grads_sem,
    parts_sem,
):
    which = 0 if first else 1
    total = lists_ref[which, 0]
    steps = (total + GROUP - 1) // GROUP

    def fetch(step, side):
        for k in range(GROUP):
            block = lists_ref[which, 1 + step * GROUP + k]
            pltpu.make_async_copy(
                weights_hbm.at[block], weights_buf.at[side, k], weights_sem.at[side, k]
            ).start()
            pltpu.make_async_copy(
                bricks_hbm.at[owner_ref[block]], bricks_buf.at[side, k], bricks_sem.at[side, k]
            ).start()

    def arrive(side):
        for k in range(GROUP):
            pltpu.make_async_copy(
                weights_hbm.at[0], weights_buf.at[side, k], weights_sem.at[side, k]
            ).wait()
            pltpu.make_async_copy(
                bricks_hbm.at[0], bricks_buf.at[side, k], bricks_sem.at[side, k]
            ).wait()

    def place(owner):
        return grads_hbm.at[owner, pl.ds(which * BLOCK, BLOCK)]

    def send(step, side):
        for k in range(GROUP):
            at = step * GROUP + k

            @pl.when(at < total)
            def _():
                owner = owner_ref[lists_ref[which, 1 + at]]
                pltpu.make_async_copy(
                    grads_buf.at[side, k], place(owner), grads_sem.at[side, k]
                ).start()

    def settle(step, side):
        for k in range(GROUP):
            at = step * GROUP + k

            @pl.when((step >= 0) & (at < total))
            def _():
                pltpu.make_async_copy(
                    grads_buf.at[side, k], place(0), grads_sem.at[side, k]
                ).wait()

    @pl.when(steps > 0)
    def _():
        fetch(0, 0)

    for ref in (acc_hid, acc_in, acc_out, acc_b_hid, acc_b_in, acc_b_out, color_ref):
        ref[...] = jnp.zeros_like(ref)
    w_in_t[...] = w_in_ref[...].T
    w_hid_t[...] = w_hid_ref[...].T
    w_out_rows[...] = jnp.zeros_like(w_out_rows)
    w_out_rows[0:4, :] = w_out_ref[...]
    d_raw_buf[...] = jnp.zeros_like(d_raw_buf)
    b_one_col[...] = jnp.broadcast_to(b_in_ref[...], (BLOCK, WIDTH)).T
    b_two_col[...] = jnp.broadcast_to(b_hid_ref[...], (BLOCK, WIDTH)).T
    for at, matrix in enumerate(lane_matrices()):
        lanes_buf[at] = matrix
    ray = lax.broadcasted_iota(jnp.int32, (BLOCK // RAY_LEN, BLOCK), 0)
    lane = lax.broadcasted_iota(jnp.int32, (BLOCK // RAY_LEN, BLOCK), 1)
    repeat = (lane // RAY_LEN == ray).astype(F32)
    for c in range(4):
        rays_buf[c] = lane_sums(rays_ref[c], repeat)

    def one_step(step, state):
        side = step % 2
        arrive(side)

        @pl.when(step + 1 < steps)
        def _():
            fetch(step + 1, 1 - side)

        for k in range(GROUP):
            at = step * GROUP + k
            block = lists_ref[which, 1 + at]
            for c in range(3):
                step_buf[c, pl.ds(k, 1), :] = rays_buf[c, pl.ds(block, 1), :]
            used = jnp.where(at < total, rays_buf[3, pl.ds(block, 1), :], 0.0)
            step_buf[3, pl.ds(k, 1), :] = used
        position = lax.broadcasted_iota(jnp.int32, (GROUP, BLOCK), 1) % RAY_LEN
        live = (position.astype(F32) < step_buf[3]).astype(F32)

        feats = jnp.concatenate(
            [dot_nt(bricks_buf[side, k], weights_buf[side, k]) for k in range(GROUP)], axis=1
        ).astype(BF16)
        pre_one = dot_nn(w_in_t[...], feats) + b_one_col[:, 0:1]
        act_one = jnp.maximum(pre_one, 0.0).astype(BF16)
        pre_two = dot_nn(w_hid_t[...], act_one) + b_two_col[:, 0:1]
        act_two = jnp.maximum(pre_two, 0.0).astype(BF16)
        raw = dot_nn(w_out_rows[...], act_two)
        for k in range(GROUP):
            for c in range(4):
                raw_buf[c, k : k + 1, :] = raw[c : c + 1, k * BLOCK : (k + 1) * BLOCK]
        colors, d_raw = render_grad(
            [raw_buf[c] + b_out_ref[c] for c in range(4)],
            live,
            [step_buf[c] for c in range(3)],
            lanes_buf[0],
            lanes_buf[1],
            lanes_buf[2],
        )
        for k in range(GROUP):
            at = step * GROUP + k
            row = jnp.where(at < total, lists_ref[which, 1 + at], BLOCK)
            for c in range(3):
                color_ref[c, pl.ds(row, 1), :] = colors[c][k : k + 1]
            for c in range(4):
                d_raw_buf[c : c + 1, k * BLOCK : (k + 1) * BLOCK] = d_raw[c][k : k + 1]
        for c in range(4):
            acc_b_out[c] += d_raw[c]
        d_raw_b = d_raw_buf[...].astype(BF16)
        acc_out[...] += dot_nt(d_raw_b, act_two)
        d_two = jnp.where(pre_two > 0.0, dot_tn(w_out_rows[...], d_raw_b), 0.0)
        d_two_b = d_two.astype(BF16)
        acc_hid[...] += dot_nt(act_one, d_two_b)
        d_one = jnp.where(pre_one > 0.0, dot_nn(w_hid_ref[...], d_two_b), 0.0)
        d_one_b = d_one.astype(BF16)
        acc_in[...] += dot_nt(feats, d_one_b)
        b_two = acc_b_hid[...]
        b_one = acc_b_in[...]
        for k in range(GROUP):
            b_two += d_two[:, k * BLOCK : (k + 1) * BLOCK]
            b_one += d_one[:, k * BLOCK : (k + 1) * BLOCK]
        acc_b_hid[...] = b_two
        acc_b_in[...] = b_one
        d_feats = dot_nn(w_in_ref[...], d_one_b).astype(BF16)
        settle(step - 2, side)
        for k in range(GROUP):
            grad = dot_nn(d_feats[:, k * BLOCK : (k + 1) * BLOCK], weights_buf[side, k])
            grad = grad.astype(BF16)
            for v in range(VOX // BLOCK):
                grads_buf[side, k, v * FEAT : (v + 1) * FEAT] = grad[:, v * BLOCK : (v + 1) * BLOCK]
        send(step, side)
        return state

    lax.fori_loop(0, steps, one_step, 0)

    ones = jnp.ones((8, BLOCK), F32)

    def over_lanes(values):
        return dot_nt(ones, values, precision=lax.Precision.HIGHEST)

    half = WIDTH // 2
    sums_ref[0:256, :] = acc_hid[:, :half]
    sums_ref[256:512, :] = acc_hid[:, half:]
    sums_ref[512:544, :] = acc_in[:, :half]
    sums_ref[544:576, :] = acc_in[:, half:]
    sums_ref[576:584, :] = acc_out[:, :half]
    sums_ref[584:592, :] = acc_out[:, half:]
    b_hid_row = over_lanes(acc_b_hid[...])
    b_in_row = over_lanes(acc_b_in[...])
    sums_ref[592:600, :] = b_hid_row[:, :half]
    sums_ref[600:608, :] = b_hid_row[:, half:]
    sums_ref[608:616, :] = b_in_row[:, :half]
    sums_ref[616:624, :] = b_in_row[:, half:]
    sums_ref[624:GRAD_ROWS, :] = jnp.zeros((GRAD_ROWS - 624, BLOCK), F32)
    for c in range(4):
        sums_ref[624 + c : 625 + c, :] = jnp.sum(acc_b_out[c], axis=0, keepdims=True)

    if not first:
        sums_ref[...] += carried_ref[...]
        sums = sums_ref[...].reshape(GRAD_ROWS // 8, 8, BLOCK)
        high = sums.astype(BF16)
        parts_buf[:, 0:8, :] = high
        parts_buf[:, 8:16, :] = (sums - high.astype(F32)).astype(BF16)
        copy = pltpu.make_async_copy(
            parts_buf, grads_hbm.at[:, pl.ds(2 * BLOCK, 16)], parts_sem
        )
        copy.start()
        copy.wait()

    settle(steps - 2, steps % 2)
    settle(steps - 1, (steps + 1) % 2)


def run_blocks(first, lists, owners, weights, bricks, rays, params, carried, grads):
    vmem = pl.BlockSpec(memory_space=pltpu.VMEM)
    smem = pl.BlockSpec(memory_space=pltpu.SMEM)
    hbm = pl.BlockSpec(memory_space=pl.ANY)
    w_in, b_in, w_hid, b_hid, w_out, b_out = params
    amount = weights.shape[0] if first else weights.shape[0] // 8
    cost = pl.CostEstimate(
        flops=amount * 70_000_000, bytes_accessed=amount * 200_000, transcendentals=amount * 1000
    )
    return pl.pallas_call(
        functools.partial(step_kernel, first),
        out_shape=(
            jax.ShapeDtypeStruct((bricks.shape[0], 2 * BLOCK + 16, BLOCK), BF16),
            jax.ShapeDtypeStruct((3, BLOCK + 8, BLOCK), F32),
            jax.ShapeDtypeStruct((GRAD_ROWS, BLOCK), F32),
        ),
        in_specs=[smem, smem, smem, hbm, hbm] + [vmem] * 7 + [hbm],
        out_specs=(hbm, vmem, vmem),
        scratch_shapes=[
            pltpu.VMEM((2, GROUP, BLOCK, VOX), BF16),
            pltpu.VMEM((2, GROUP, FEAT, VOX), BF16),
            pltpu.VMEM((2, GROUP, BLOCK, BLOCK), BF16),
            pltpu.VMEM((4, BLOCK, BLOCK), F32),
            pltpu.VMEM((4, GROUP, BLOCK), F32),
            pltpu.VMEM((8, GROUP * BLOCK), F32),
            pltpu.VMEM((4, GROUP, BLOCK), F32),
            pltpu.VMEM((3, BLOCK, BLOCK), F32),
            pltpu.VMEM((WIDTH, FEAT), BF16),
            pltpu.VMEM((WIDTH, WIDTH), BF16),
            pltpu.VMEM((8, WIDTH), BF16),
            pltpu.VMEM((WIDTH, BLOCK), F32),
            pltpu.VMEM((WIDTH, BLOCK), F32),
            pltpu.VMEM((WIDTH, WIDTH), F32),
            pltpu.VMEM((FEAT, WIDTH), F32),
            pltpu.VMEM((8, WIDTH), F32),
            pltpu.VMEM((WIDTH, BLOCK), F32),
            pltpu.VMEM((WIDTH, BLOCK), F32),
            pltpu.VMEM((4, GROUP, BLOCK), F32),
            pltpu.VMEM((GRAD_ROWS // 8, 16, BLOCK), BF16),
            pltpu.SemaphoreType.DMA((2, GROUP)),
            pltpu.SemaphoreType.DMA((2, GROUP)),
            pltpu.SemaphoreType.DMA((2, GROUP)),
            pltpu.SemaphoreType.DMA,
        ],
        compiler_params=pltpu.CompilerParams(vmem_limit_bytes=60 << 20),
        input_output_aliases={} if first else {12: 0},
        cost_estimate=cost,
        name="blocks_first" if first else "blocks_second",
    )(
        lists,
        owners,
        b_out,
        weights,
        bricks,
        rays,
        w_in,
        b_in[None],
        w_hid,
        b_hid[None],
        w_out,
        carried,
        grads,
    )


TAKE = 8


def collect_kernel(ids_ref, grads_ref, out_ref):
    step = pl.program_id(0)

    @pl.when(step == 0)
    def _():
        out_ref[...] = jnp.zeros_like(out_ref)

    for k in range(TAKE):
        for r in range(2):
            brick = ids_ref[2 * (step * TAKE + k) + r]

            @pl.when(brick >= 0)
            def _():
                for v in range(VOX // BLOCK):
                    rows = pl.ds(r * BLOCK + v * FEAT, FEAT)
                    out_ref[brick, :, v * BLOCK : (v + 1) * BLOCK] += grads_ref[k, rows].astype(F32)


def collect(ids, grads, own):
    amount, rows, _ = grads.shape
    return pl.pallas_call(
        collect_kernel,
        out_shape=jax.ShapeDtypeStruct((own, FEAT, VOX), F32),
        grid_spec=pltpu.PrefetchScalarGridSpec(
            num_scalar_prefetch=1,
            grid=(amount // TAKE,),
            in_specs=[pl.BlockSpec((TAKE, rows, BLOCK), lambda i, ids: (i, 0, 0))],
            out_specs=pl.BlockSpec((own, FEAT, VOX), lambda i, ids: (0, 0, 0)),
        ),
        compiler_params=pltpu.CompilerParams(vmem_limit_bytes=60 << 20),
        cost_estimate=pl.CostEstimate(
            flops=amount * FEAT * VOX, bytes_accessed=amount * FEAT * VOX * 4, transcendentals=0
        ),
        name="collect",
    )(ids, grads)


def exchange(values):
    return lax.all_to_all(values, AXES, split_axis=0, concat_axis=0, tiled=True)


def body(
    brick_feats,
    interp_weights,
    block_owner,
    block_brick,
    sample_count,
    target,
    w_in,
    b_in,
    w_hid,
    b_hid,
    w_out,
    b_out,
):
    own_blocks = interp_weights.shape[0]
    own_bricks = brick_feats.shape[0]
    dev_count = lax.axis_size(AXES)
    owners = block_owner[:, 0]
    wish, lists = plan(owners, block_brick[:, 0], dev_count)
    asked = exchange(wish.reshape(dev_count, 1, 2)).reshape(dev_count, 2)

    bricks_t = jnp.swapaxes(brick_feats, 1, 2)
    fetched = [exchange(bricks_t[jnp.maximum(asked[:, r], 0)]) for r in range(2)]

    rays = jnp.concatenate([target, sample_count.astype(F32)[None]])
    rays = rays.reshape(4, own_blocks, BLOCK // RAY_LEN)
    params = (w_in, b_in, w_hid, b_hid, w_out, b_out)
    nothing = jnp.zeros((8, BLOCK), F32)
    grads, color_0, sums = run_blocks(
        True, lists, owners, interp_weights, fetched[0], rays, params, nothing, nothing
    )
    grads, color_1, _ = run_blocks(
        False, lists, owners, interp_weights, fetched[1], rays, params, sums, grads
    )
    returned = exchange(grads)

    parts = returned[:, 2 * BLOCK :].astype(F32)
    mine = jnp.sum(parts[:, :8] + parts[:, 8:], axis=0)
    totals = exchange(jnp.broadcast_to(mine[None], (dev_count, 8, BLOCK)))
    brick_grad = jnp.swapaxes(collect(asked.reshape(-1), returned, own_bricks), 1, 2)

    totals = totals.reshape(GRAD_ROWS, BLOCK) / (sample_count.shape[0] * dev_count)

    def joined(start, rows):
        return jnp.concatenate([totals[start : start + rows], totals[start + rows : start + 2 * rows]], axis=1)

    g_w_hid = joined(0, WIDTH)
    g_w_in = joined(2 * WIDTH, FEAT)
    g_w_out = joined(576, 8)[:4]
    g_b_hid = joined(592, 8)[0]
    g_b_in = joined(608, 8)[0]
    g_b_out = jnp.sum(totals[624:628], axis=1)
    color = (color_0 + color_1)[:, :own_blocks, ::RAY_LEN].reshape(3, -1)
    return (brick_grad, color, g_w_in, g_b_in, g_w_hid, g_b_hid, g_w_out, g_b_out)


def solution(mesh):
    shared = P(AXES, None, None)
    return jax.shard_map(
        body,
        mesh=mesh,
        in_specs=(
            shared,
            shared,
            P(AXES, None),
            P(AXES, None),
            P(AXES),
            P(None, AXES),
            P(),
            P(),
            P(),
            P(),
            P(),
            P(),
        ),
        out_specs=(shared, P(None, AXES), P(), P(), P(), P(), P(), P()),
        check_vma=False,
    )
```

```python
import functools

import jax
import jax.numpy as jnp
from jax import lax
from jax.experimental import pallas as pl
from jax.experimental.pallas import tpu as pltpu
from jax.sharding import PartitionSpec as P


FEAT = 32
VOX = 512
WIDTH = 256
BLOCK = 128
RAY_LEN = 32
GROUP = 8
GRAD_ROWS = 1024
VMEM_LIMIT = 60 << 20

AXES = ("view", "space")
step_len = 0.05
F32 = jnp.float32
BF16 = jnp.bfloat16


def dot_nn(left, right, precision=None):
    return lax.dot_general(
        left, right, (((1,), (0,)), ((), ())), precision=precision, preferred_element_type=F32
    )


def dot_nt(left, right, precision=None):
    return lax.dot_general(
        left, right, (((1,), (1,)), ((), ())), precision=precision, preferred_element_type=F32
    )


def dot_tn(left, right):
    return lax.dot_general(
        left, right, (((0,), (0,)), ((), ())), preferred_element_type=F32
    )


def lane_sums(values, matrix):
    return dot_nn(values, matrix, precision=lax.Precision.HIGHEST)


def render_grad(raw, live, goal, before, within, after):
    rows = live.shape[0]
    small = jnp.exp(-jnp.abs(raw[0]))
    sigma = jnp.maximum(raw[0], 0.0) + jnp.log1p(small)
    slope = jnp.where(raw[0] >= 0.0, 1.0, small) / (1.0 + small)
    shades = [jax.nn.sigmoid(channel) for channel in raw[1:]]
    depth = step_len * sigma * live
    faded = jnp.exp(-depth)
    trans = jnp.exp(depth - lane_sums(depth, before))
    weight = trans * (1.0 - faded)
    stacked = jnp.concatenate([weight * shade for shade in shades], axis=0)
    color = lane_sums(stacked, within)
    colors = [color[c * rows : (c + 1) * rows] for c in range(3)]
    miss = [colors[c] - goal[c] for c in range(3)]
    d_weight = miss[0] * shades[0] + miss[1] * shades[1] + miss[2] * shades[2]
    d_depth = d_weight * (trans * faded) - lane_sums(d_weight * weight, after)
    d_raw = [step_len * live * d_depth * slope]
    for c in range(3):
        d_raw.append(weight * miss[c] * shades[c] * (1.0 - shades[c]))
    return colors, d_raw


def lane_matrices():
    row = lax.broadcasted_iota(jnp.int32, (BLOCK, BLOCK), 0)
    col = lax.broadcasted_iota(jnp.int32, (BLOCK, BLOCK), 1)
    same = (row // RAY_LEN) == (col // RAY_LEN)
    before = (same & (row <= col)).astype(F32)
    after = (same & (row > col)).astype(F32)
    return before, same.astype(F32), after


def plan_kernel(owner_ref, brick_ref, wish_ref, lists_ref):
    amount = owner_ref.shape[0]

    def clear(i, state):
        wish_ref[2 * i] = -1
        wish_ref[2 * i + 1] = -1
        return state

    lax.fori_loop(0, wish_ref.shape[0] // 2, clear, 0, unroll=8)

    def place(i, state):
        firsts, seconds = state
        owner = owner_ref[i]
        rank = jnp.where(wish_ref[2 * owner] >= 0, 1, 0)
        wish_ref[2 * owner + rank] = brick_ref[i]
        lists_ref[0, 1 + firsts] = i
        lists_ref[1, 1 + seconds] = i
        return firsts + 1 - rank, seconds + rank

    counts = lax.fori_loop(0, amount, place, (0, 0), unroll=4)
    for rank in range(2):
        lists_ref[rank, 0] = counts[rank]
        for k in range(GROUP):
            lists_ref[rank, 1 + counts[rank] + k] = 0


def plan(owners, bricks, dev_count):
    smem = pl.BlockSpec(memory_space=pltpu.SMEM)
    return pl.pallas_call(
        plan_kernel,
        out_shape=(
            jax.ShapeDtypeStruct((dev_count * 2,), jnp.int32),
            jax.ShapeDtypeStruct((2, owners.shape[0] + 2 * GROUP), jnp.int32),
        ),
        in_specs=[smem, smem],
        out_specs=(smem, smem),
        name="plan",
    )(owners, bricks)


def step_kernel(
    first,
    lists_ref,
    owner_ref,
    b_out_ref,
    weights_hbm,
    bricks_hbm,
    rays_ref,
    w_in_ref,
    b_in_ref,
    w_hid_ref,
    b_hid_ref,
    w_out_ref,
    carried_ref,
    grads_hbm,
    color_ref,
    sums_ref,
    weights_buf,
    bricks_buf,
    grads_buf,
    raw_buf,
    d_raw_buf,
    step_buf,
    lanes_buf,
    w_in_t,
    w_hid_t,
    w_out_rows,
    b_one_col,
    b_two_col,
    acc_hid,
    acc_in,
    acc_out,
    acc_b_hid,
    acc_b_in,
    acc_b_out,
    parts_buf,
    weights_sem,
    bricks_sem,
    grads_sem,
    parts_sem,
):
    which = 0 if first else 1
    total = lists_ref[which, 0]
    steps = (total + GROUP - 1) // GROUP

    def fetch(step, side):
        for k in range(GROUP):
            block = lists_ref[which, 1 + step * GROUP + k]
            pltpu.make_async_copy(
                weights_hbm.at[block], weights_buf.at[side, k], weights_sem.at[side, k]
            ).start()
            pltpu.make_async_copy(
                bricks_hbm.at[owner_ref[block]], bricks_buf.at[side, k], bricks_sem.at[side, k]
            ).start()

    def arrive(side):
        for k in range(GROUP):
            pltpu.make_async_copy(
                weights_hbm.at[0], weights_buf.at[side, k], weights_sem.at[side, k]
            ).wait()
            pltpu.make_async_copy(
                bricks_hbm.at[0], bricks_buf.at[side, k], bricks_sem.at[side, k]
            ).wait()

    def place(owner):
        return grads_hbm.at[owner, pl.ds(0, BLOCK)]

    def send(step, side):
        for k in range(GROUP):
            at = step * GROUP + k

            @pl.when(at < total)
            def _():
                owner = owner_ref[lists_ref[which, 1 + at]]
                pltpu.make_async_copy(
                    grads_buf.at[side, k], place(owner), grads_sem.at[side, k]
                ).start()

    def settle(step, side):
        for k in range(GROUP):
            at = step * GROUP + k

            @pl.when((step >= 0) & (at < total))
            def _():
                pltpu.make_async_copy(
                    grads_buf.at[side, k], place(0), grads_sem.at[side, k]
                ).wait()

    @pl.when(steps > 0)
    def _():
        fetch(0, 0)

    for ref in (acc_hid, acc_in, acc_out, acc_b_hid, acc_b_in, acc_b_out, color_ref):
        ref[...] = jnp.zeros_like(ref)
    w_in_t[...] = w_in_ref[...].T
    w_hid_t[...] = w_hid_ref[...].T
    w_out_rows[...] = jnp.zeros_like(w_out_rows)
    w_out_rows[0:4, :] = w_out_ref[...]
    d_raw_buf[...] = jnp.zeros_like(d_raw_buf)
    b_one_col[...] = jnp.broadcast_to(b_in_ref[...], (BLOCK, WIDTH)).T
    b_two_col[...] = jnp.broadcast_to(b_hid_ref[...], (BLOCK, WIDTH)).T
    for at, matrix in enumerate(lane_matrices()):
        lanes_buf[at] = matrix

    def one_step(step, state):
        side = step % 2
        arrive(side)

        @pl.when(step + 1 < steps)
        def _():
            fetch(step + 1, 1 - side)

        for k in range(GROUP):
            at = step * GROUP + k
            block = lists_ref[which, 1 + at]
            for c in range(3):
                step_buf[c, pl.ds(k, 1), :] = rays_ref[c, pl.ds(block, 1), :]
            used = jnp.where(at < total, rays_ref[3, pl.ds(block, 1), :], 0.0)
            step_buf[3, pl.ds(k, 1), :] = used
        position = lax.broadcasted_iota(jnp.int32, (GROUP, BLOCK), 1) % RAY_LEN
        live = (position.astype(F32) < step_buf[3]).astype(F32)

        feats = jnp.concatenate(
            [dot_nt(bricks_buf[side, k], weights_buf[side, k]) for k in range(GROUP)], axis=1
        ).astype(BF16)
        pre_one = dot_nn(w_in_t[...], feats) + b_one_col[:, 0:1]
        act_one = jnp.maximum(pre_one, 0.0).astype(BF16)
        pre_two = dot_nn(w_hid_t[...], act_one) + b_two_col[:, 0:1]
        act_two = jnp.maximum(pre_two, 0.0).astype(BF16)
        raw = dot_nn(w_out_rows[...], act_two)
        for k in range(GROUP):
            for c in range(4):
                raw_buf[c, k : k + 1, :] = raw[c : c + 1, k * BLOCK : (k + 1) * BLOCK]
        colors, d_raw = render_grad(
            [raw_buf[c] + b_out_ref[c] for c in range(4)],
            live,
            [step_buf[c] for c in range(3)],
            lanes_buf[0],
            lanes_buf[1],
            lanes_buf[2],
        )
        for k in range(GROUP):
            at = step * GROUP + k
            row = jnp.where(at < total, lists_ref[which, 1 + at], BLOCK)
            for c in range(3):
                color_ref[c, pl.ds(row, 1), :] = colors[c][k : k + 1]
            for c in range(4):
                d_raw_buf[c : c + 1, k * BLOCK : (k + 1) * BLOCK] = d_raw[c][k : k + 1]
        for c in range(4):
            acc_b_out[c] += d_raw[c]
        d_raw_b = d_raw_buf[...].astype(BF16)
        acc_out[...] += dot_nt(d_raw_b, act_two)
        d_two = jnp.where(pre_two > 0.0, dot_tn(w_out_rows[...], d_raw_b), 0.0)
        d_two_b = d_two.astype(BF16)
        acc_hid[...] += dot_nt(act_one, d_two_b)
        d_one = jnp.where(pre_one > 0.0, dot_nn(w_hid_ref[...], d_two_b), 0.0)
        d_one_b = d_one.astype(BF16)
        acc_in[...] += dot_nt(feats, d_one_b)
        b_two = acc_b_hid[...]
        b_one = acc_b_in[...]
        for k in range(GROUP):
            b_two += d_two[:, k * BLOCK : (k + 1) * BLOCK]
            b_one += d_one[:, k * BLOCK : (k + 1) * BLOCK]
        acc_b_hid[...] = b_two
        acc_b_in[...] = b_one
        d_feats = dot_nn(w_in_ref[...], d_one_b).astype(BF16)
        settle(step - 2, side)
        for k in range(GROUP):
            grad = dot_nn(d_feats[:, k * BLOCK : (k + 1) * BLOCK], weights_buf[side, k])
            grad = grad.astype(BF16)
            for v in range(VOX // BLOCK):
                grads_buf[side, k, v * FEAT : (v + 1) * FEAT] = grad[:, v * BLOCK : (v + 1) * BLOCK]
        send(step, side)
        return state

    lax.fori_loop(0, steps, one_step, 0)

    ones = jnp.ones((8, BLOCK), F32)

    def over_lanes(values):
        return dot_nt(ones, values, precision=lax.Precision.HIGHEST)

    half = WIDTH // 2
    sums_ref[0:256, :] = acc_hid[:, :half]
    sums_ref[256:512, :] = acc_hid[:, half:]
    sums_ref[512:544, :] = acc_in[:, :half]
    sums_ref[544:576, :] = acc_in[:, half:]
    sums_ref[576:584, :] = acc_out[:, :half]
    sums_ref[584:592, :] = acc_out[:, half:]
    b_hid_row = over_lanes(acc_b_hid[...])
    b_in_row = over_lanes(acc_b_in[...])
    sums_ref[592:600, :] = b_hid_row[:, :half]
    sums_ref[600:608, :] = b_hid_row[:, half:]
    sums_ref[608:616, :] = b_in_row[:, :half]
    sums_ref[616:624, :] = b_in_row[:, half:]
    sums_ref[624:GRAD_ROWS, :] = jnp.zeros((GRAD_ROWS - 624, BLOCK), F32)
    for c in range(4):
        sums_ref[624 + c : 625 + c, :] = jnp.sum(acc_b_out[c], axis=0, keepdims=True)

    if not first:
        sums_ref[...] += carried_ref[...]
        sums = sums_ref[...].reshape(GRAD_ROWS // 8, 8, BLOCK)
        high = sums.astype(BF16)
        parts_buf[:, 0:8, :] = high
        parts_buf[:, 8:16, :] = (sums - high.astype(F32)).astype(BF16)
        copy = pltpu.make_async_copy(
            parts_buf, grads_hbm.at[:, pl.ds(BLOCK, 16)], parts_sem
        )
        copy.start()
        copy.wait()

    settle(steps - 2, steps % 2)
    settle(steps - 1, (steps + 1) % 2)


def expand_kernel(rays_ref, out_ref):
    ray = lax.broadcasted_iota(jnp.int32, (BLOCK // RAY_LEN, BLOCK), 0)
    lane = lax.broadcasted_iota(jnp.int32, (BLOCK // RAY_LEN, BLOCK), 1)
    repeat = (lane // RAY_LEN == ray).astype(F32)
    for c in range(4):
        out_ref[c] = lane_sums(rays_ref[c], repeat)


def expand(rays):
    channels, blocks, _ = rays.shape
    return pl.pallas_call(
        expand_kernel,
        out_shape=jax.ShapeDtypeStruct((channels, blocks, BLOCK), F32),
        in_specs=[pl.BlockSpec(memory_space=pltpu.VMEM)],
        out_specs=pl.BlockSpec(memory_space=pltpu.VMEM),
        cost_estimate=pl.CostEstimate(flops=1_000_000, bytes_accessed=300_000, transcendentals=0),
        name="expand",
    )(rays)


def run_blocks(first, lists, owners, weights, bricks, rays, params, carried):
    vmem = pl.BlockSpec(memory_space=pltpu.VMEM)
    smem = pl.BlockSpec(memory_space=pltpu.SMEM)
    hbm = pl.BlockSpec(memory_space=pl.ANY)
    w_in, b_in, w_hid, b_hid, w_out, b_out = params
    amount = weights.shape[0] if first else weights.shape[0] // 8
    cost = pl.CostEstimate(
        flops=amount * 70_000_000, bytes_accessed=amount * 200_000, transcendentals=amount * 1000
    )
    return pl.pallas_call(
        functools.partial(step_kernel, first),
        out_shape=(
            jax.ShapeDtypeStruct((bricks.shape[0], BLOCK + (0 if first else 16), BLOCK), BF16),
            jax.ShapeDtypeStruct((3, BLOCK + 8, BLOCK), F32),
            jax.ShapeDtypeStruct((GRAD_ROWS, BLOCK), F32),
        ),
        in_specs=[smem, smem, smem, hbm, hbm] + [vmem] * 7,
        out_specs=(hbm, vmem, vmem),
        scratch_shapes=[
            pltpu.VMEM((2, GROUP, BLOCK, VOX), BF16),
            pltpu.VMEM((2, GROUP, FEAT, VOX), BF16),
            pltpu.VMEM((2, GROUP, BLOCK, BLOCK), BF16),
            pltpu.VMEM((4, GROUP, BLOCK), F32),
            pltpu.VMEM((8, GROUP * BLOCK), F32),
            pltpu.VMEM((4, GROUP, BLOCK), F32),
            pltpu.VMEM((3, BLOCK, BLOCK), F32),
            pltpu.VMEM((WIDTH, FEAT), BF16),
            pltpu.VMEM((WIDTH, WIDTH), BF16),
            pltpu.VMEM((8, WIDTH), BF16),
            pltpu.VMEM((WIDTH, BLOCK), F32),
            pltpu.VMEM((WIDTH, BLOCK), F32),
            pltpu.VMEM((WIDTH, WIDTH), F32),
            pltpu.VMEM((FEAT, WIDTH), F32),
            pltpu.VMEM((8, WIDTH), F32),
            pltpu.VMEM((WIDTH, BLOCK), F32),
            pltpu.VMEM((WIDTH, BLOCK), F32),
            pltpu.VMEM((4, GROUP, BLOCK), F32),
            pltpu.VMEM((GRAD_ROWS // 8, 16, BLOCK), BF16),
            pltpu.SemaphoreType.DMA((2, GROUP)),
            pltpu.SemaphoreType.DMA((2, GROUP)),
            pltpu.SemaphoreType.DMA((2, GROUP)),
            pltpu.SemaphoreType.DMA,
        ],
        compiler_params=pltpu.CompilerParams(vmem_limit_bytes=VMEM_LIMIT),
        cost_estimate=cost,
        name="blocks_first" if first else "blocks_second",
    )(
        lists,
        owners,
        b_out,
        weights,
        bricks,
        rays,
        w_in,
        b_in[None],
        w_hid,
        b_hid[None],
        w_out,
        carried,
    )


TAKE = 16


def collect_kernel(first, ids_ref, grads_ref, carried_ref, out_ref):
    step = pl.program_id(0)

    @pl.when(step == 0)
    def _():
        if first:
            out_ref[...] = jnp.zeros_like(out_ref)
        else:
            out_ref[...] = carried_ref[...]

    for k in range(TAKE):
        brick = ids_ref[step * TAKE + k]

        @pl.when(brick >= 0)
        def _():
            for v in range(VOX // BLOCK):
                rows = grads_ref[k, v * FEAT : (v + 1) * FEAT].astype(F32)
                out_ref[brick, :, v * BLOCK : (v + 1) * BLOCK] += rows


def collect(ids, grads, own, carried):
    amount, rows, _ = grads.shape
    first = carried is None
    if first:
        carried = jnp.zeros((8, BLOCK), F32)
        held = pl.BlockSpec((8, BLOCK), lambda i, ids: (0, 0))
    else:
        held = pl.BlockSpec((own, FEAT, VOX), lambda i, ids: (0, 0, 0), pipeline_mode=pl.Buffered(1))
    return pl.pallas_call(
        functools.partial(collect_kernel, first),
        out_shape=jax.ShapeDtypeStruct((own, FEAT, VOX), F32),
        grid_spec=pltpu.PrefetchScalarGridSpec(
            num_scalar_prefetch=1,
            grid=(amount // TAKE,),
            in_specs=[pl.BlockSpec((TAKE, rows, BLOCK), lambda i, ids: (i, 0, 0)), held],
            out_specs=pl.BlockSpec((own, FEAT, VOX), lambda i, ids: (0, 0, 0)),
        ),
        compiler_params=pltpu.CompilerParams(vmem_limit_bytes=VMEM_LIMIT),
        cost_estimate=pl.CostEstimate(
            flops=amount * FEAT * VOX, bytes_accessed=amount * FEAT * VOX * 4, transcendentals=0
        ),
        name="collect_first" if first else "collect_second",
    )(ids, grads, carried)


def exchange(values):
    return lax.all_to_all(values, AXES, split_axis=0, concat_axis=0, tiled=True)


def body(
    brick_feats,
    interp_weights,
    block_owner,
    block_brick,
    sample_count,
    target,
    w_in,
    b_in,
    w_hid,
    b_hid,
    w_out,
    b_out,
):
    own_blocks = interp_weights.shape[0]
    own_bricks = brick_feats.shape[0]
    dev_count = lax.axis_size(AXES)
    owners = block_owner[:, 0]
    wish, lists = plan(owners, block_brick[:, 0], dev_count)
    asked = exchange(wish.reshape(dev_count, 1, 2)).reshape(dev_count, 2)

    bricks_t = jnp.swapaxes(brick_feats, 1, 2)
    fetched = [exchange(bricks_t[jnp.maximum(asked[:, r], 0)]) for r in range(2)]

    rays = jnp.concatenate([target, sample_count.astype(F32)[None]])
    rays = expand(rays.reshape(4, own_blocks, BLOCK // RAY_LEN))
    params = (w_in, b_in, w_hid, b_hid, w_out, b_out)
    nothing = jnp.zeros((8, BLOCK), F32)
    grads_0, color_0, sums = run_blocks(
        True, lists, owners, interp_weights, fetched[0], rays, params, nothing
    )
    grads_1, color_1, _ = run_blocks(
        False, lists, owners, interp_weights, fetched[1], rays, params, sums
    )
    returned_0 = exchange(grads_0)
    returned_1 = exchange(grads_1)
    partial = collect(asked[:, 0], returned_0, own_bricks, None)

    parts = returned_1[:, BLOCK:].astype(F32)
    mine = jnp.sum(parts[:, :8] + parts[:, 8:], axis=0)
    totals = exchange(jnp.broadcast_to(mine[None], (dev_count, 8, BLOCK)))
    brick_grad = collect(asked[:, 1], returned_1, own_bricks, partial)
    brick_grad = jnp.swapaxes(brick_grad, 1, 2)

    totals = totals.reshape(GRAD_ROWS, BLOCK) / (sample_count.shape[0] * dev_count)

    def joined(start, rows):
        return jnp.concatenate([totals[start : start + rows], totals[start + rows : start + 2 * rows]], axis=1)

    g_w_hid = joined(0, WIDTH)
    g_w_in = joined(2 * WIDTH, FEAT)
    g_w_out = joined(576, 8)[:4]
    g_b_hid = joined(592, 8)[0]
    g_b_in = joined(608, 8)[0]
    g_b_out = jnp.sum(totals[624:628], axis=1)
    color = (color_0 + color_1)[:, :own_blocks, ::RAY_LEN].reshape(3, -1)
    return (brick_grad, color, g_w_in, g_b_in, g_w_hid, g_b_hid, g_w_out, g_b_out)


def solution(mesh):
    shared = P(AXES, None, None)
    return jax.shard_map(
        body,
        mesh=mesh,
        in_specs=(
            shared,
            shared,
            P(AXES, None),
            P(AXES, None),
            P(AXES),
            P(None, AXES),
            P(),
            P(),
            P(),
            P(),
            P(),
            P(),
        ),
        out_specs=(shared, P(None, AXES), P(), P(), P(), P(), P(), P()),
        check_vma=False,
    )
```

```python
import functools

import jax
import jax.numpy as jnp
from jax import lax
from jax.experimental import pallas as pl
from jax.experimental.pallas import tpu as pltpu
from jax.sharding import PartitionSpec as P


FEAT = 32
VOX = 512
WIDTH = 256
BLOCK = 128
RAY_LEN = 32
GROUP = 16
GRAD_ROWS = 1024
VMEM_LIMIT = 66_000_000

AXES = ("view", "space")
step_len = 0.05
F32 = jnp.float32
BF16 = jnp.bfloat16


def dot_nn(left, right, precision=None):
    return lax.dot_general(
        left, right, (((1,), (0,)), ((), ())), precision=precision, preferred_element_type=F32
    )


def dot_nt(left, right, precision=None):
    return lax.dot_general(
        left, right, (((1,), (1,)), ((), ())), precision=precision, preferred_element_type=F32
    )


def dot_tn(left, right):
    return lax.dot_general(
        left, right, (((0,), (0,)), ((), ())), preferred_element_type=F32
    )


def lane_sums(values, matrix):
    return dot_nn(values, matrix, precision=lax.Precision.HIGHEST)


def render_grad(raw, live, goal, before, within, after):
    rows = live.shape[0]
    small = jnp.exp(-jnp.abs(raw[0]))
    sigma = jnp.maximum(raw[0], 0.0) + jnp.log1p(small)
    slope = jnp.where(raw[0] >= 0.0, 1.0, small) / (1.0 + small)
    shades = [jax.nn.sigmoid(channel) for channel in raw[1:]]
    depth = step_len * sigma * live
    faded = jnp.exp(-depth)
    trans = jnp.exp(depth - lane_sums(depth, before))
    weight = trans * (1.0 - faded)
    stacked = jnp.concatenate([weight * shade for shade in shades], axis=0)
    color = lane_sums(stacked, within)
    colors = [color[c * rows : (c + 1) * rows] for c in range(3)]
    miss = [colors[c] - goal[c] for c in range(3)]
    d_weight = miss[0] * shades[0] + miss[1] * shades[1] + miss[2] * shades[2]
    d_depth = d_weight * (trans * faded) - lane_sums(d_weight * weight, after)
    d_raw = [step_len * live * d_depth * slope]
    for c in range(3):
        d_raw.append(weight * miss[c] * shades[c] * (1.0 - shades[c]))
    return colors, d_raw


def lane_matrices():
    row = lax.broadcasted_iota(jnp.int32, (BLOCK, BLOCK), 0)
    col = lax.broadcasted_iota(jnp.int32, (BLOCK, BLOCK), 1)
    same = (row // RAY_LEN) == (col // RAY_LEN)
    before = (same & (row <= col)).astype(F32)
    after = (same & (row > col)).astype(F32)
    return before, same.astype(F32), after


def plan_kernel(owner_ref, brick_ref, wish_ref, lists_ref):
    amount = owner_ref.shape[0]

    half = wish_ref.shape[0] // 2

    def clear(i, state):
        wish_ref[i] = -1
        wish_ref[half + i] = -1
        return state

    lax.fori_loop(0, half, clear, 0, unroll=8)

    def place(i, state):
        firsts, seconds = state
        owner = owner_ref[i]
        rank = jnp.where(wish_ref[owner] >= 0, 1, 0)
        wish_ref[half * rank + owner] = brick_ref[i]
        lists_ref[0, 1 + firsts] = i
        lists_ref[1, 1 + seconds] = i
        return firsts + 1 - rank, seconds + rank

    counts = lax.fori_loop(0, amount, place, (0, 0), unroll=4)
    for rank in range(2):
        lists_ref[rank, 0] = counts[rank]
        for k in range(GROUP):
            lists_ref[rank, 1 + counts[rank] + k] = 0


def plan(owners, bricks, dev_count):
    smem = pl.BlockSpec(memory_space=pltpu.SMEM)
    return pl.pallas_call(
        plan_kernel,
        out_shape=(
            jax.ShapeDtypeStruct((dev_count * 2,), jnp.int32),
            jax.ShapeDtypeStruct((2, owners.shape[0] + 2 * GROUP), jnp.int32),
        ),
        in_specs=[smem, smem],
        out_specs=(smem, smem),
        name="plan",
    )(owners, bricks)


def step_kernel(
    first,
    stride,
    lists_ref,
    owner_ref,
    b_out_ref,
    weights_hbm,
    bricks_hbm,
    rays_ref,
    w_in_ref,
    b_in_ref,
    w_hid_ref,
    b_hid_ref,
    w_out_ref,
    carried_ref,
    grads_hbm,
    color_ref,
    sums_ref,
    weights_buf,
    bricks_buf,
    grads_buf,
    raw_buf,
    d_raw_buf,
    step_buf,
    lanes_buf,
    w_in_t,
    w_hid_t,
    w_out_rows,
    b_one_col,
    b_two_col,
    acc_hid,
    acc_in,
    acc_out,
    acc_b_hid,
    acc_b_in,
    acc_b_out,
    parts_buf,
    weights_sem,
    bricks_sem,
    grads_sem,
    parts_sem,
):
    which = 0 if first else 1
    parts = 1 if stride is None else 2
    feats_each, rows_each = FEAT // parts, BLOCK // parts
    total = lists_ref[which, 0]

    def mate(owner, part):
        if stride is None:
            return owner
        return owner + (part - owner // stride % 2) * stride

    steps = (total + GROUP - 1) // GROUP

    def fetch(step, side):
        for k in range(GROUP):
            block = lists_ref[which, 1 + step * GROUP + k]
            pltpu.make_async_copy(
                weights_hbm.at[block], weights_buf.at[side, k], weights_sem.at[side, k]
            ).start()
            owner = owner_ref[block]
            for part in range(parts):
                pltpu.make_async_copy(
                    bricks_hbm.at[mate(owner, part)],
                    bricks_buf.at[side, k, pl.ds(part * feats_each, feats_each)],
                    bricks_sem.at[side, k, part],
                ).start()

    def arrive(side):
        for k in range(GROUP):
            pltpu.make_async_copy(
                weights_hbm.at[0], weights_buf.at[side, k], weights_sem.at[side, k]
            ).wait()
            for part in range(parts):
                pltpu.make_async_copy(
                    bricks_hbm.at[0],
                    bricks_buf.at[side, k, pl.ds(part * feats_each, feats_each)],
                    bricks_sem.at[side, k, part],
                ).wait()

    def leave(side, k, part, owner):
        return pltpu.make_async_copy(
            grads_buf.at[side, k, pl.ds(part * rows_each, rows_each)],
            grads_hbm.at[mate(owner, part), pl.ds(0, rows_each)],
            grads_sem.at[side, k, part],
        )

    def send(step, side):
        for k in range(GROUP):
            at = step * GROUP + k

            @pl.when(at < total)
            def _():
                owner = owner_ref[lists_ref[which, 1 + at]]
                for part in range(parts):
                    leave(side, k, part, owner).start()

    def settle(step, side):
        for k in range(GROUP):
            at = step * GROUP + k

            @pl.when((step >= 0) & (at < total))
            def _():
                for part in range(parts):
                    leave(side, k, part, 0).wait()

    @pl.when(steps > 0)
    def _():
        fetch(0, 0)

    for ref in (acc_hid, acc_in, acc_out, acc_b_hid, acc_b_in, acc_b_out, color_ref):
        ref[...] = jnp.zeros_like(ref)
    w_in_t[...] = w_in_ref[...].T
    w_hid_t[...] = w_hid_ref[...].T
    w_out_rows[...] = jnp.zeros_like(w_out_rows)
    w_out_rows[0:4, :] = w_out_ref[...]
    d_raw_buf[...] = jnp.zeros_like(d_raw_buf)
    b_one_col[...] = jnp.broadcast_to(b_in_ref[...], (BLOCK, WIDTH)).T
    b_two_col[...] = jnp.broadcast_to(b_hid_ref[...], (BLOCK, WIDTH)).T
    for at, matrix in enumerate(lane_matrices()):
        lanes_buf[at] = matrix

    def one_step(step, state):
        side = step % 2
        arrive(side)

        @pl.when(step + 1 < steps)
        def _():
            fetch(step + 1, 1 - side)

        for k in range(GROUP):
            at = step * GROUP + k
            block = lists_ref[which, 1 + at]
            for c in range(3):
                step_buf[c, pl.ds(k, 1), :] = rays_ref[c, pl.ds(block, 1), :]
            used = jnp.where(at < total, rays_ref[3, pl.ds(block, 1), :], 0.0)
            step_buf[3, pl.ds(k, 1), :] = used
        position = lax.broadcasted_iota(jnp.int32, (GROUP, BLOCK), 1) % RAY_LEN
        live = (position.astype(F32) < step_buf[3]).astype(F32)

        feats = jnp.concatenate(
            [dot_nt(bricks_buf[side, k], weights_buf[side, k]) for k in range(GROUP)], axis=1
        ).astype(BF16)
        pre_one = dot_nn(w_in_t[...], feats) + b_one_col[:, 0:1]
        act_one = jnp.maximum(pre_one, 0.0).astype(BF16)
        pre_two = dot_nn(w_hid_t[...], act_one) + b_two_col[:, 0:1]
        act_two = jnp.maximum(pre_two, 0.0).astype(BF16)
        raw = dot_nn(w_out_rows[...], act_two)
        for k in range(GROUP):
            for c in range(4):
                raw_buf[c, k : k + 1, :] = raw[c : c + 1, k * BLOCK : (k + 1) * BLOCK]
        colors, d_raw = render_grad(
            [raw_buf[c] + b_out_ref[c] for c in range(4)],
            live,
            [step_buf[c] for c in range(3)],
            lanes_buf[0],
            lanes_buf[1],
            lanes_buf[2],
        )
        for k in range(GROUP):
            at = step * GROUP + k
            row = jnp.where(at < total, lists_ref[which, 1 + at], BLOCK)
            for c in range(3):
                color_ref[c, pl.ds(row, 1), :] = colors[c][k : k + 1]
            for c in range(4):
                d_raw_buf[c : c + 1, k * BLOCK : (k + 1) * BLOCK] = d_raw[c][k : k + 1]
        for c in range(4):
            acc_b_out[c] += d_raw[c]
        d_raw_b = d_raw_buf[...].astype(BF16)
        acc_out[...] += dot_nt(d_raw_b, act_two)
        d_two = jnp.where(pre_two > 0.0, dot_tn(w_out_rows[...], d_raw_b), 0.0)
        d_two_b = d_two.astype(BF16)
        acc_hid[...] += dot_nt(act_one, d_two_b)
        d_one = jnp.where(pre_one > 0.0, dot_nn(w_hid_ref[...], d_two_b), 0.0)
        d_one_b = d_one.astype(BF16)
        acc_in[...] += dot_nt(feats, d_one_b)
        b_two = acc_b_hid[...]
        b_one = acc_b_in[...]
        for k in range(GROUP):
            b_two += d_two[:, k * BLOCK : (k + 1) * BLOCK]
            b_one += d_one[:, k * BLOCK : (k + 1) * BLOCK]
        acc_b_hid[...] = b_two
        acc_b_in[...] = b_one
        d_feats = dot_nn(w_in_ref[...], d_one_b).astype(BF16)
        settle(step - 2, side)
        for k in range(GROUP):
            grad = dot_nn(d_feats[:, k * BLOCK : (k + 1) * BLOCK], weights_buf[side, k])
            grad = grad.astype(BF16)
            for part in range(parts):
                feat = part * feats_each
                for v in range(VOX // BLOCK):
                    row = part * rows_each + v * feats_each
                    grads_buf[side, k, row : row + feats_each] = grad[
                        feat : feat + feats_each, v * BLOCK : (v + 1) * BLOCK
                    ]
        send(step, side)
        return state

    lax.fori_loop(0, steps, one_step, 0)

    ones = jnp.ones((8, BLOCK), F32)

    def over_lanes(values):
        return dot_nt(ones, values, precision=lax.Precision.HIGHEST)

    half = WIDTH // 2
    sums_ref[0:256, :] = acc_hid[:, :half]
    sums_ref[256:512, :] = acc_hid[:, half:]
    sums_ref[512:544, :] = acc_in[:, :half]
    sums_ref[544:576, :] = acc_in[:, half:]
    sums_ref[576:584, :] = acc_out[:, :half]
    sums_ref[584:592, :] = acc_out[:, half:]
    b_hid_row = over_lanes(acc_b_hid[...])
    b_in_row = over_lanes(acc_b_in[...])
    sums_ref[592:600, :] = b_hid_row[:, :half]
    sums_ref[600:608, :] = b_hid_row[:, half:]
    sums_ref[608:616, :] = b_in_row[:, :half]
    sums_ref[616:624, :] = b_in_row[:, half:]
    sums_ref[624:GRAD_ROWS, :] = jnp.zeros((GRAD_ROWS - 624, BLOCK), F32)
    for c in range(4):
        sums_ref[624 + c : 625 + c, :] = jnp.sum(acc_b_out[c], axis=0, keepdims=True)

    if not first:
        sums_ref[...] += carried_ref[...]
        sums = sums_ref[...].reshape(GRAD_ROWS // 8, 8, BLOCK)
        high = sums.astype(BF16)
        parts_buf[:, 0:8, :] = high
        parts_buf[:, 8:16, :] = (sums - high.astype(F32)).astype(BF16)
        copy = pltpu.make_async_copy(
            parts_buf, grads_hbm.at[:, pl.ds(rows_each, 16)], parts_sem
        )
        copy.start()
        copy.wait()

    settle(steps - 2, steps % 2)
    settle(steps - 1, (steps + 1) % 2)


def expand_kernel(rays_ref, out_ref):
    ray = lax.broadcasted_iota(jnp.int32, (BLOCK // RAY_LEN, BLOCK), 0)
    lane = lax.broadcasted_iota(jnp.int32, (BLOCK // RAY_LEN, BLOCK), 1)
    repeat = (lane // RAY_LEN == ray).astype(F32)
    for c in range(4):
        out_ref[c] = lane_sums(rays_ref[c], repeat)


def expand(rays):
    channels, blocks, _ = rays.shape
    return pl.pallas_call(
        expand_kernel,
        out_shape=jax.ShapeDtypeStruct((channels, blocks, BLOCK), F32),
        in_specs=[pl.BlockSpec(memory_space=pltpu.VMEM)],
        out_specs=pl.BlockSpec(memory_space=pltpu.VMEM),
        cost_estimate=pl.CostEstimate(flops=1_000_000, bytes_accessed=300_000, transcendentals=0),
        name="expand",
    )(rays)


def run_blocks(first, lists, owners, weights, bricks, rays, params, carried, stride=None):
    vmem = pl.BlockSpec(memory_space=pltpu.VMEM)
    smem = pl.BlockSpec(memory_space=pltpu.SMEM)
    hbm = pl.BlockSpec(memory_space=pl.ANY)
    w_in, b_in, w_hid, b_hid, w_out, b_out = params
    amount = weights.shape[0] if first else weights.shape[0] // 8
    parts = 1 if stride is None else 2
    rows = BLOCK // parts + (0 if first else 16)
    cost = pl.CostEstimate(
        flops=amount * 70_000_000, bytes_accessed=amount * 200_000, transcendentals=amount * 1000
    )
    return pl.pallas_call(
        functools.partial(step_kernel, first, stride),
        out_shape=(
            jax.ShapeDtypeStruct((bricks.shape[0], rows, BLOCK), BF16),
            jax.ShapeDtypeStruct((3, BLOCK + 8, BLOCK), F32),
            jax.ShapeDtypeStruct((GRAD_ROWS, BLOCK), F32),
        ),
        in_specs=[smem, smem, smem, hbm, hbm] + [vmem] * 7,
        out_specs=(hbm, vmem, vmem),
        scratch_shapes=[
            pltpu.VMEM((2, GROUP, BLOCK, VOX), BF16),
            pltpu.VMEM((2, GROUP, FEAT, VOX), BF16),
            pltpu.VMEM((2, GROUP, BLOCK, BLOCK), BF16),
            pltpu.VMEM((4, GROUP, BLOCK), F32),
            pltpu.VMEM((8, GROUP * BLOCK), F32),
            pltpu.VMEM((4, GROUP, BLOCK), F32),
            pltpu.VMEM((3, BLOCK, BLOCK), F32),
            pltpu.VMEM((WIDTH, FEAT), BF16),
            pltpu.VMEM((WIDTH, WIDTH), BF16),
            pltpu.VMEM((8, WIDTH), BF16),
            pltpu.VMEM((WIDTH, BLOCK), F32),
            pltpu.VMEM((WIDTH, BLOCK), F32),
            pltpu.VMEM((WIDTH, WIDTH), F32),
            pltpu.VMEM((FEAT, WIDTH), F32),
            pltpu.VMEM((8, WIDTH), F32),
            pltpu.VMEM((WIDTH, BLOCK), F32),
            pltpu.VMEM((WIDTH, BLOCK), F32),
            pltpu.VMEM((4, GROUP, BLOCK), F32),
            pltpu.VMEM((GRAD_ROWS // 8, 16, BLOCK), BF16),
            pltpu.SemaphoreType.DMA((2, GROUP)),
            pltpu.SemaphoreType.DMA((2, GROUP, parts)),
            pltpu.SemaphoreType.DMA((2, GROUP, parts)),
            pltpu.SemaphoreType.DMA,
        ],
        compiler_params=pltpu.CompilerParams(vmem_limit_bytes=VMEM_LIMIT),
        cost_estimate=cost,
    )(
        lists,
        owners,
        b_out,
        weights,
        bricks,
        rays,
        w_in,
        b_in[None],
        w_hid,
        b_hid[None],
        w_out,
        carried,
    )


TAKE = 16


def collect_kernel(first, ids_ref, grads_ref, carried_ref, out_ref):
    step = pl.program_id(0)

    @pl.when(step == 0)
    def _():
        if first:
            out_ref[...] = jnp.zeros_like(out_ref)
        else:
            out_ref[...] = carried_ref[...]

    for k in range(TAKE):
        brick = ids_ref[step * TAKE + k]

        @pl.when(brick >= 0)
        def _():
            for v in range(VOX // BLOCK):
                rows = grads_ref[k, v * FEAT : (v + 1) * FEAT].astype(F32)
                out_ref[brick, :, v * BLOCK : (v + 1) * BLOCK] += rows


def collect(ids, grads, own, carried):
    amount, rows, _ = grads.shape
    first = carried is None
    if first:
        carried = jnp.zeros((8, BLOCK), F32)
        held = pl.BlockSpec((8, BLOCK), lambda i, ids: (0, 0))
    else:
        held = pl.BlockSpec((own, FEAT, VOX), lambda i, ids: (0, 0, 0), pipeline_mode=pl.Buffered(1))
    return pl.pallas_call(
        functools.partial(collect_kernel, first),
        out_shape=jax.ShapeDtypeStruct((own, FEAT, VOX), F32),
        grid_spec=pltpu.PrefetchScalarGridSpec(
            num_scalar_prefetch=1,
            grid=(amount // TAKE,),
            in_specs=[pl.BlockSpec((TAKE, rows, BLOCK), lambda i, ids: (i, 0, 0)), held],
            out_specs=pl.BlockSpec((own, FEAT, VOX), lambda i, ids: (0, 0, 0)),
        ),
        compiler_params=pltpu.CompilerParams(vmem_limit_bytes=VMEM_LIMIT),
        cost_estimate=pl.CostEstimate(
            flops=amount * FEAT * VOX, bytes_accessed=amount * FEAT * VOX * 4, transcendentals=0
        ),
        name="collect_first" if first else "collect_second",
    )(ids, grads, carried)


def collect_halves_kernel(ids_ref, grads_ref, carried_ref, out_ref, mate_ref):
    step = pl.program_id(0)
    own = out_ref.shape[0]
    half = FEAT // 2
    feat = pl.multiple_of(ids_ref[ids_ref.shape[0] - 1] * half, half)

    @pl.when(step == 0)
    def _():
        out_ref[...] = carried_ref[...]
        mate_ref[...] = jnp.zeros_like(mate_ref)

    for k in range(TAKE):
        brick = ids_ref[step * TAKE + k]

        @pl.when((brick >= 0) & (brick < own))
        def _():
            for v in range(VOX // BLOCK):
                rows = grads_ref[k, v * half : (v + 1) * half].astype(F32)
                out_ref[brick, pl.ds(feat, half), v * BLOCK : (v + 1) * BLOCK] += rows

        @pl.when(brick >= own)
        def _():
            for v in range(VOX // BLOCK):
                rows = grads_ref[k, v * half : (v + 1) * half].astype(F32)
                mate_ref[brick - own, :, v * BLOCK : (v + 1) * BLOCK] += rows


def collect_halves(ids, grads, own, carried):
    amount, rows, _ = grads.shape
    half = FEAT // 2
    return pl.pallas_call(
        collect_halves_kernel,
        out_shape=(
            jax.ShapeDtypeStruct((own, FEAT, VOX), F32),
            jax.ShapeDtypeStruct((own, half, VOX), F32),
        ),
        grid_spec=pltpu.PrefetchScalarGridSpec(
            num_scalar_prefetch=1,
            grid=(amount // TAKE,),
            in_specs=[
                pl.BlockSpec((TAKE, rows, BLOCK), lambda i, ids: (i, 0, 0)),
                pl.BlockSpec(
                    (own, FEAT, VOX), lambda i, ids: (0, 0, 0), pipeline_mode=pl.Buffered(1)
                ),
            ],
            out_specs=(
                pl.BlockSpec((own, FEAT, VOX), lambda i, ids: (0, 0, 0)),
                pl.BlockSpec((own, half, VOX), lambda i, ids: (0, 0, 0)),
            ),
        ),
        compiler_params=pltpu.CompilerParams(vmem_limit_bytes=VMEM_LIMIT),
        cost_estimate=pl.CostEstimate(
            flops=amount * FEAT * VOX, bytes_accessed=amount * FEAT * VOX * 4, transcendentals=0
        ),
        name="collect_halves",
    )(ids, grads, carried)


MERGE = 16


def merge_kernel(core_ref, sums_ref, arrived_ref, out_ref):
    half = FEAT // 2
    feat = pl.multiple_of((1 - core_ref[0]) * half, half)
    out_ref[...] = sums_ref[...]
    out_ref[:, pl.ds(feat, half), :] += arrived_ref[...]


def merge(core, sums, arrived):
    own, half, _ = arrived.shape
    whole = pl.BlockSpec((MERGE, FEAT, VOX), lambda i, core: (i, 0, 0))
    return pl.pallas_call(
        merge_kernel,
        out_shape=jax.ShapeDtypeStruct(sums.shape, F32),
        grid_spec=pltpu.PrefetchScalarGridSpec(
            num_scalar_prefetch=1,
            grid=(own // MERGE,),
            in_specs=[whole, pl.BlockSpec((MERGE, half, VOX), lambda i, core: (i, 0, 0))],
            out_specs=whole,
        ),
        compiler_params=pltpu.CompilerParams(vmem_limit_bytes=VMEM_LIMIT),
        name="merge",
    )(core, sums, arrived)


def exchange(values):
    return lax.all_to_all(values, AXES, split_axis=0, concat_axis=0, tiled=True)


def body(
    brick_feats,
    interp_weights,
    block_owner,
    block_brick,
    sample_count,
    target,
    w_in,
    b_in,
    w_hid,
    b_hid,
    w_out,
    b_out,
):
    own_blocks = interp_weights.shape[0]
    own_bricks = brick_feats.shape[0]
    dev_count = lax.axis_size(AXES)
    owners = block_owner[:, 0]
    space = lax.axis_size("space")
    me = lax.axis_index(AXES)
    core = lax.axis_index("view") % 2
    wish, lists = plan(owners, block_brick[:, 0], dev_count)
    wishes = exchange(jnp.broadcast_to(wish.reshape(1, 2, dev_count), (dev_count, 2, dev_count)))
    asked = [wishes[:, r, :] for r in range(2)]
    mine = [lax.dynamic_index_in_dim(a, me, axis=1, keepdims=False) for a in asked]
    other = me + (1 - 2 * core) * space
    others = lax.dynamic_index_in_dim(asked[1], other, axis=1, keepdims=False)
    others = jnp.where(others >= 0, others + own_bricks, -1)
    halves = jnp.where(mine[1] >= 0, mine[1], others)
    twice = (asked[1] >= 0).reshape(dev_count, dev_count // (2 * space), 2, space)
    crowded = jnp.any(twice[:, :, 0] & twice[:, :, 1])

    bricks_t = jnp.swapaxes(brick_feats, 1, 2)
    half = FEAT // 2
    swap = [(v, v ^ 1) for v in range(lax.axis_size("view"))]

    def part(which):
        return lax.dynamic_slice_in_dim(bricks_t, which * half, half, axis=1)

    chip_bricks = jnp.concatenate([part(core), lax.ppermute(part(1 - core), "view", swap)])
    fetched_0 = exchange(bricks_t[jnp.maximum(mine[0], 0)])
    sent_wholes = bricks_t[jnp.maximum(mine[1], 0)]
    sent_halves = chip_bricks[jnp.maximum(halves, 0)]
    sent_wholes, sent_halves = lax.optimization_barrier((sent_wholes, sent_halves))

    rays = jnp.concatenate([target, sample_count.astype(F32)[None]])
    rays = expand(rays.reshape(4, own_blocks, BLOCK // RAY_LEN))
    params = (w_in, b_in, w_hid, b_hid, w_out, b_out)
    nothing = jnp.zeros((8, BLOCK), F32)

    def rest(split, fetched_0, sent_1, ids_1, core, lists, owners, weights, rays, ids_0):
        stride = space if split else None
        rows = BLOCK // 2 if split else BLOCK
        fetched_1 = exchange(sent_1)
        grads_0, color_0, sums = run_blocks(
            True, lists, owners, weights, fetched_0, rays, params, nothing
        )
        grads_1, color_1, _ = run_blocks(
            False, lists, owners, weights, fetched_1, rays, params, sums, stride
        )
        returned_0 = exchange(grads_0)
        returned_1 = exchange(grads_1)
        partial = collect(ids_0, returned_0, own_bricks, None)
        parts = returned_1[:, rows:].astype(F32)
        chunk = jnp.sum(parts[:, :8] + parts[:, 8:], axis=0)
        totals = exchange(jnp.broadcast_to(chunk[None], (dev_count, 8, BLOCK)))
        if split:
            grad, spare = collect_halves(
                jnp.concatenate([ids_1, core[None]]), returned_1, own_bricks, partial
            )
            grad = merge(core[None], grad, lax.ppermute(spare, "view", swap))
        else:
            grad = collect(ids_1, returned_1, own_bricks, partial)
        color = (color_0 + color_1)[:, :own_blocks, ::RAY_LEN].reshape(3, -1)
        return grad, color, totals

    common = (lists, owners, interp_weights, rays, mine[0])
    brick_grad, color, totals = lax.cond(
        crowded,
        lambda f, full, split, *c: rest(False, f, full, mine[1], core, *c),
        lambda f, full, split, *c: rest(True, f, split, halves, core, *c),
        fetched_0,
        sent_wholes,
        sent_halves,
        *common,
    )
    brick_grad = jnp.swapaxes(brick_grad, 1, 2)

    totals = totals.reshape(GRAD_ROWS, BLOCK) / (sample_count.shape[0] * dev_count)

    def joined(start, rows):
        return jnp.concatenate([totals[start : start + rows], totals[start + rows : start + 2 * rows]], axis=1)

    g_w_hid = joined(0, WIDTH)
    g_w_in = joined(2 * WIDTH, FEAT)
    g_w_out = joined(576, 8)[:4]
    g_b_hid = joined(592, 8)[0]
    g_b_in = joined(608, 8)[0]
    g_b_out = jnp.sum(totals[624:628], axis=1)
    return (brick_grad, color, g_w_in, g_b_in, g_w_hid, g_b_hid, g_w_out, g_b_out)


def solution(mesh):
    shared = P(AXES, None, None)
    return jax.shard_map(
        body,
        mesh=mesh,
        in_specs=(
            shared,
            shared,
            P(AXES, None),
            P(AXES, None),
            P(AXES),
            P(None, AXES),
            P(),
            P(),
            P(),
            P(),
            P(),
            P(),
        ),
        out_specs=(shared, P(None, AXES), P(), P(), P(), P(), P(), P()),
        check_vma=False,
    )
```

```python
import functools

import jax
import jax.numpy as jnp
from jax import lax
from jax.experimental import pallas as pl
from jax.experimental.pallas import tpu as pltpu
from jax.sharding import PartitionSpec as P


FEAT = 32
VOX = 512
WIDTH = 256
BLOCK = 128
RAY_LEN = 32
GROUP = 16
GRAD_ROWS = 1024
VMEM_LIMIT = 66_000_000

AXES = ("view", "space")
step_len = 0.05
F32 = jnp.float32
BF16 = jnp.bfloat16


def dot_nn(left, right, precision=None):
    return lax.dot_general(
        left, right, (((1,), (0,)), ((), ())), precision=precision, preferred_element_type=F32
    )


def dot_nt(left, right, precision=None):
    return lax.dot_general(
        left, right, (((1,), (1,)), ((), ())), precision=precision, preferred_element_type=F32
    )


def dot_tn(left, right):
    return lax.dot_general(
        left, right, (((0,), (0,)), ((), ())), preferred_element_type=F32
    )


def lane_sums(values, matrix):
    return dot_nn(values, matrix, precision=lax.Precision.HIGHEST)


def render_grad(raw, live, goal, before, within, after):
    rows = live.shape[0]
    small = jnp.exp(-jnp.abs(raw[0]))
    sigma = jnp.maximum(raw[0], 0.0) + jnp.log1p(small)
    slope = jnp.where(raw[0] >= 0.0, 1.0, small) / (1.0 + small)
    shades = [jax.nn.sigmoid(channel) for channel in raw[1:]]
    depth = step_len * sigma * live
    faded = jnp.exp(-depth)
    trans = jnp.exp(depth - lane_sums(depth, before))
    weight = trans * (1.0 - faded)
    stacked = jnp.concatenate([weight * shade for shade in shades], axis=0)
    color = lane_sums(stacked, within)
    colors = [color[c * rows : (c + 1) * rows] for c in range(3)]
    miss = [colors[c] - goal[c] for c in range(3)]
    d_weight = miss[0] * shades[0] + miss[1] * shades[1] + miss[2] * shades[2]
    d_depth = d_weight * (trans * faded) - lane_sums(d_weight * weight, after)
    d_raw = [step_len * live * d_depth * slope]
    for c in range(3):
        d_raw.append(weight * miss[c] * shades[c] * (1.0 - shades[c]))
    return colors, d_raw


def lane_matrices():
    row = lax.broadcasted_iota(jnp.int32, (BLOCK, BLOCK), 0)
    col = lax.broadcasted_iota(jnp.int32, (BLOCK, BLOCK), 1)
    same = (row // RAY_LEN) == (col // RAY_LEN)
    before = (same & (row <= col)).astype(F32)
    after = (same & (row > col)).astype(F32)
    return before, same.astype(F32), after


def plan_kernel(owner_ref, brick_ref, wish_ref, lists_ref):
    amount = owner_ref.shape[0]

    half = wish_ref.shape[0] // 2

    def clear(i, state):
        wish_ref[i] = -1
        wish_ref[half + i] = -1
        return state

    lax.fori_loop(0, half, clear, 0, unroll=8)

    def place(i, state):
        firsts, seconds = state
        owner = owner_ref[i]
        rank = jnp.where(wish_ref[owner] >= 0, 1, 0)
        wish_ref[half * rank + owner] = brick_ref[i]
        lists_ref[0, 1 + firsts] = i
        lists_ref[1, 1 + seconds] = i
        return firsts + 1 - rank, seconds + rank

    counts = lax.fori_loop(0, amount, place, (0, 0), unroll=4)
    for rank in range(2):
        lists_ref[rank, 0] = counts[rank]
        for k in range(GROUP):
            lists_ref[rank, 1 + counts[rank] + k] = 0


def plan(owners, bricks, dev_count):
    smem = pl.BlockSpec(memory_space=pltpu.SMEM)
    return pl.pallas_call(
        plan_kernel,
        out_shape=(
            jax.ShapeDtypeStruct((dev_count * 2,), jnp.int32),
            jax.ShapeDtypeStruct((2, owners.shape[0] + 2 * GROUP), jnp.int32),
        ),
        in_specs=[smem, smem],
        out_specs=(smem, smem),
        name="plan",
    )(owners, bricks)


def step_kernel(
    first,
    stride,
    lists_ref,
    owner_ref,
    b_out_ref,
    weights_hbm,
    bricks_hbm,
    rays_ref,
    w_in_ref,
    b_in_ref,
    w_hid_ref,
    b_hid_ref,
    w_out_ref,
    carried_ref,
    grads_hbm,
    color_ref,
    sums_ref,
    weights_buf,
    bricks_buf,
    grads_buf,
    raw_buf,
    d_raw_buf,
    step_buf,
    lanes_buf,
    w_in_t,
    w_hid_t,
    w_out_rows,
    b_one_col,
    b_two_col,
    acc_hid,
    acc_in,
    acc_out,
    acc_b_hid,
    acc_b_in,
    acc_b_out,
    parts_buf,
    weights_sem,
    bricks_sem,
    grads_sem,
    parts_sem,
):
    which = 0 if first else 1
    parts = 1 if stride is None else 2
    feats_each, rows_each = FEAT // parts, BLOCK // parts
    total = lists_ref[which, 0]

    def mate(owner, part):
        if stride is None:
            return owner
        return owner + (part - owner // stride % 2) * stride

    steps = (total + GROUP - 1) // GROUP

    def fetch(step, side):
        for k in range(GROUP):
            block = lists_ref[which, 1 + step * GROUP + k]
            pltpu.make_async_copy(
                weights_hbm.at[block], weights_buf.at[side, k], weights_sem.at[side, k]
            ).start()
            owner = owner_ref[block]
            for part in range(parts):
                pltpu.make_async_copy(
                    bricks_hbm.at[mate(owner, part)],
                    bricks_buf.at[side, k, pl.ds(part * feats_each, feats_each)],
                    bricks_sem.at[side, k, part],
                ).start()

    def arrive(side):
        for k in range(GROUP):
            pltpu.make_async_copy(
                weights_hbm.at[0], weights_buf.at[side, k], weights_sem.at[side, k]
            ).wait()
            for part in range(parts):
                pltpu.make_async_copy(
                    bricks_hbm.at[0],
                    bricks_buf.at[side, k, pl.ds(part * feats_each, feats_each)],
                    bricks_sem.at[side, k, part],
                ).wait()

    def leave(side, k, part, owner):
        return pltpu.make_async_copy(
            grads_buf.at[side, k, pl.ds(part * rows_each, rows_each)],
            grads_hbm.at[mate(owner, part), pl.ds(0, rows_each)],
            grads_sem.at[side, k, part],
        )

    def send(step, side):
        for k in range(GROUP):
            at = step * GROUP + k

            @pl.when(at < total)
            def _():
                owner = owner_ref[lists_ref[which, 1 + at]]
                for part in range(parts):
                    leave(side, k, part, owner).start()

    def settle(step, side):
        for k in range(GROUP):
            at = step * GROUP + k

            @pl.when((step >= 0) & (at < total))
            def _():
                for part in range(parts):
                    leave(side, k, part, 0).wait()

    @pl.when(steps > 0)
    def _():
        fetch(0, 0)

    for ref in (acc_hid, acc_in, acc_out, acc_b_hid, acc_b_in, acc_b_out, color_ref):
        ref[...] = jnp.zeros_like(ref)
    w_in_t[...] = w_in_ref[...].T
    w_hid_t[...] = w_hid_ref[...].T
    w_out_rows[...] = jnp.zeros_like(w_out_rows)
    w_out_rows[0:4, :] = w_out_ref[...]
    d_raw_buf[...] = jnp.zeros_like(d_raw_buf)
    b_one_col[...] = jnp.broadcast_to(b_in_ref[...], (BLOCK, WIDTH)).T
    b_two_col[...] = jnp.broadcast_to(b_hid_ref[...], (BLOCK, WIDTH)).T
    for at, matrix in enumerate(lane_matrices()):
        lanes_buf[at] = matrix

    def one_step(step, state):
        side = step % 2
        arrive(side)

        @pl.when(step + 1 < steps)
        def _():
            fetch(step + 1, 1 - side)

        for k in range(GROUP):
            at = step * GROUP + k
            block = lists_ref[which, 1 + at]
            for c in range(3):
                step_buf[c, pl.ds(k, 1), :] = rays_ref[c, pl.ds(block, 1), :]
            used = jnp.where(at < total, rays_ref[3, pl.ds(block, 1), :], 0.0)
            step_buf[3, pl.ds(k, 1), :] = used
        position = lax.broadcasted_iota(jnp.int32, (GROUP, BLOCK), 1) % RAY_LEN
        live = (position.astype(F32) < step_buf[3]).astype(F32)

        feats = jnp.concatenate(
            [dot_nt(bricks_buf[side, k], weights_buf[side, k]) for k in range(GROUP)], axis=1
        ).astype(BF16)
        pre_one = dot_nn(w_in_t[...], feats) + b_one_col[:, 0:1]
        act_one = jnp.maximum(pre_one, 0.0).astype(BF16)
        pre_two = dot_nn(w_hid_t[...], act_one) + b_two_col[:, 0:1]
        act_two = jnp.maximum(pre_two, 0.0).astype(BF16)
        raw = dot_nn(w_out_rows[...], act_two)
        for k in range(GROUP):
            for c in range(4):
                raw_buf[c, k : k + 1, :] = raw[c : c + 1, k * BLOCK : (k + 1) * BLOCK]
        colors, d_raw = render_grad(
            [raw_buf[c] + b_out_ref[c] for c in range(4)],
            live,
            [step_buf[c] for c in range(3)],
            lanes_buf[0],
            lanes_buf[1],
            lanes_buf[2],
        )
        for k in range(GROUP):
            at = step * GROUP + k
            row = jnp.where(at < total, lists_ref[which, 1 + at], BLOCK)
            for c in range(3):
                color_ref[c, pl.ds(row, 1), :] = colors[c][k : k + 1]
            for c in range(4):
                d_raw_buf[c : c + 1, k * BLOCK : (k + 1) * BLOCK] = d_raw[c][k : k + 1]
        for c in range(4):
            acc_b_out[c] += d_raw[c]
        d_raw_b = d_raw_buf[...].astype(BF16)
        acc_out[...] += dot_nt(d_raw_b, act_two)
        d_two = jnp.where(pre_two > 0.0, dot_tn(w_out_rows[...], d_raw_b), 0.0)
        d_two_b = d_two.astype(BF16)
        acc_hid[...] += dot_nt(act_one, d_two_b)
        d_one = jnp.where(pre_one > 0.0, dot_nn(w_hid_ref[...], d_two_b), 0.0)
        d_one_b = d_one.astype(BF16)
        acc_in[...] += dot_nt(feats, d_one_b)
        b_two = acc_b_hid[...]
        b_one = acc_b_in[...]
        for k in range(GROUP):
            b_two += d_two[:, k * BLOCK : (k + 1) * BLOCK]
            b_one += d_one[:, k * BLOCK : (k + 1) * BLOCK]
        acc_b_hid[...] = b_two
        acc_b_in[...] = b_one
        d_feats = dot_nn(w_in_ref[...], d_one_b).astype(BF16)
        settle(step - 2, side)
        for k in range(GROUP):
            grad = dot_nn(d_feats[:, k * BLOCK : (k + 1) * BLOCK], weights_buf[side, k])
            grad = grad.astype(BF16)
            for part in range(parts):
                feat = part * feats_each
                for v in range(VOX // BLOCK):
                    row = part * rows_each + v * feats_each
                    grads_buf[side, k, row : row + feats_each] = grad[
                        feat : feat + feats_each, v * BLOCK : (v + 1) * BLOCK
                    ]
        send(step, side)
        return state

    lax.fori_loop(0, steps, one_step, 0)

    ones = jnp.ones((8, BLOCK), F32)

    def over_lanes(values):
        return dot_nt(ones, values, precision=lax.Precision.HIGHEST)

    half = WIDTH // 2
    sums_ref[0:256, :] = acc_hid[:, :half]
    sums_ref[256:512, :] = acc_hid[:, half:]
    sums_ref[512:544, :] = acc_in[:, :half]
    sums_ref[544:576, :] = acc_in[:, half:]
    sums_ref[576:584, :] = acc_out[:, :half]
    sums_ref[584:592, :] = acc_out[:, half:]
    b_hid_row = over_lanes(acc_b_hid[...])
    b_in_row = over_lanes(acc_b_in[...])
    sums_ref[592:600, :] = b_hid_row[:, :half]
    sums_ref[600:608, :] = b_hid_row[:, half:]
    sums_ref[608:616, :] = b_in_row[:, :half]
    sums_ref[616:624, :] = b_in_row[:, half:]
    sums_ref[624:GRAD_ROWS, :] = jnp.zeros((GRAD_ROWS - 624, BLOCK), F32)
    for c in range(4):
        sums_ref[624 + c : 625 + c, :] = jnp.sum(acc_b_out[c], axis=0, keepdims=True)

    if not first:
        sums_ref[...] += carried_ref[...]
        sums = sums_ref[...].reshape(GRAD_ROWS // 8, 8, BLOCK)
        high = sums.astype(BF16)
        parts_buf[:, 0:8, :] = high
        parts_buf[:, 8:16, :] = (sums - high.astype(F32)).astype(BF16)
        copy = pltpu.make_async_copy(
            parts_buf, grads_hbm.at[:, pl.ds(rows_each, 16)], parts_sem
        )
        copy.start()
        copy.wait()

    settle(steps - 2, steps % 2)
    settle(steps - 1, (steps + 1) % 2)


def expand_kernel(rays_ref, out_ref):
    ray = lax.broadcasted_iota(jnp.int32, (BLOCK // RAY_LEN, BLOCK), 0)
    lane = lax.broadcasted_iota(jnp.int32, (BLOCK // RAY_LEN, BLOCK), 1)
    repeat = (lane // RAY_LEN == ray).astype(F32)
    for c in range(4):
        out_ref[c] = lane_sums(rays_ref[c], repeat)


def expand(rays):
    channels, blocks, _ = rays.shape
    return pl.pallas_call(
        expand_kernel,
        out_shape=jax.ShapeDtypeStruct((channels, blocks, BLOCK), F32),
        in_specs=[pl.BlockSpec(memory_space=pltpu.VMEM)],
        out_specs=pl.BlockSpec(memory_space=pltpu.VMEM),
        cost_estimate=pl.CostEstimate(flops=1_000_000, bytes_accessed=300_000, transcendentals=0),
        name="expand",
    )(rays)


def run_blocks(first, lists, owners, weights, bricks, rays, params, carried, stride=None):
    vmem = pl.BlockSpec(memory_space=pltpu.VMEM)
    smem = pl.BlockSpec(memory_space=pltpu.SMEM)
    hbm = pl.BlockSpec(memory_space=pl.ANY)
    w_in, b_in, w_hid, b_hid, w_out, b_out = params
    amount = weights.shape[0] if first else weights.shape[0] // 8
    parts = 1 if stride is None else 2
    rows = BLOCK // parts + (0 if first else 16)
    cost = pl.CostEstimate(
        flops=amount * 70_000_000, bytes_accessed=amount * 200_000, transcendentals=amount * 1000
    )
    return pl.pallas_call(
        functools.partial(step_kernel, first, stride),
        out_shape=(
            jax.ShapeDtypeStruct((bricks.shape[0], rows, BLOCK), BF16),
            jax.ShapeDtypeStruct((3, BLOCK + 8, BLOCK), F32),
            jax.ShapeDtypeStruct((GRAD_ROWS, BLOCK), F32),
        ),
        in_specs=[smem, smem, smem, hbm, hbm] + [vmem] * 7,
        out_specs=(hbm, vmem, vmem),
        scratch_shapes=[
            pltpu.VMEM((2, GROUP, BLOCK, VOX), BF16),
            pltpu.VMEM((2, GROUP, FEAT, VOX), BF16),
            pltpu.VMEM((2, GROUP, BLOCK, BLOCK), BF16),
            pltpu.VMEM((4, GROUP, BLOCK), F32),
            pltpu.VMEM((8, GROUP * BLOCK), F32),
            pltpu.VMEM((4, GROUP, BLOCK), F32),
            pltpu.VMEM((3, BLOCK, BLOCK), F32),
            pltpu.VMEM((WIDTH, FEAT), BF16),
            pltpu.VMEM((WIDTH, WIDTH), BF16),
            pltpu.VMEM((8, WIDTH), BF16),
            pltpu.VMEM((WIDTH, BLOCK), F32),
            pltpu.VMEM((WIDTH, BLOCK), F32),
            pltpu.VMEM((WIDTH, WIDTH), F32),
            pltpu.VMEM((FEAT, WIDTH), F32),
            pltpu.VMEM((8, WIDTH), F32),
            pltpu.VMEM((WIDTH, BLOCK), F32),
            pltpu.VMEM((WIDTH, BLOCK), F32),
            pltpu.VMEM((4, GROUP, BLOCK), F32),
            pltpu.VMEM((GRAD_ROWS // 8, 16, BLOCK), BF16),
            pltpu.SemaphoreType.DMA((2, GROUP)),
            pltpu.SemaphoreType.DMA((2, GROUP, parts)),
            pltpu.SemaphoreType.DMA((2, GROUP, parts)),
            pltpu.SemaphoreType.DMA,
        ],
        compiler_params=pltpu.CompilerParams(vmem_limit_bytes=VMEM_LIMIT),
        cost_estimate=cost,
    )(
        lists,
        owners,
        b_out,
        weights,
        bricks,
        rays,
        w_in,
        b_in[None],
        w_hid,
        b_hid[None],
        w_out,
        carried,
    )


TAKE = 16


def collect_kernel(first, ids_ref, grads_ref, carried_ref, out_ref):
    step = pl.program_id(0)

    @pl.when(step == 0)
    def _():
        if first:
            out_ref[...] = jnp.zeros_like(out_ref)
        else:
            out_ref[...] = carried_ref[...]

    for k in range(TAKE):
        brick = ids_ref[step * TAKE + k]

        @pl.when(brick >= 0)
        def _():
            for v in range(VOX // BLOCK):
                rows = grads_ref[k, v * FEAT : (v + 1) * FEAT].astype(F32)
                out_ref[brick, :, v * BLOCK : (v + 1) * BLOCK] += rows


def collect(ids, grads, own, carried):
    amount, rows, _ = grads.shape
    first = carried is None
    if first:
        carried = jnp.zeros((8, BLOCK), F32)
        held = pl.BlockSpec((8, BLOCK), lambda i, ids: (0, 0))
    else:
        held = pl.BlockSpec((own, FEAT, VOX), lambda i, ids: (0, 0, 0), pipeline_mode=pl.Buffered(1))
    return pl.pallas_call(
        functools.partial(collect_kernel, first),
        out_shape=jax.ShapeDtypeStruct((own, FEAT, VOX), F32),
        grid_spec=pltpu.PrefetchScalarGridSpec(
            num_scalar_prefetch=1,
            grid=(amount // TAKE,),
            in_specs=[pl.BlockSpec((TAKE, rows, BLOCK), lambda i, ids: (i, 0, 0)), held],
            out_specs=pl.BlockSpec((own, FEAT, VOX), lambda i, ids: (0, 0, 0)),
        ),
        compiler_params=pltpu.CompilerParams(vmem_limit_bytes=VMEM_LIMIT),
        cost_estimate=pl.CostEstimate(
            flops=amount * FEAT * VOX, bytes_accessed=amount * FEAT * VOX * 4, transcendentals=0
        ),
        name="collect_first" if first else "collect_second",
    )(ids, grads, carried)


def collect_halves_kernel(ids_ref, grads_ref, carried_ref, out_ref, mate_ref):
    step = pl.program_id(0)
    own = out_ref.shape[0]
    half = FEAT // 2
    feat = pl.multiple_of(ids_ref[ids_ref.shape[0] - 1] * half, half)

    @pl.when(step == 0)
    def _():
        out_ref[...] = carried_ref[...]
        mate_ref[...] = jnp.zeros_like(mate_ref)

    for k in range(TAKE):
        brick = ids_ref[step * TAKE + k]

        @pl.when((brick >= 0) & (brick < own))
        def _():
            for v in range(VOX // BLOCK):
                rows = grads_ref[k, v * half : (v + 1) * half].astype(F32)
                out_ref[brick, pl.ds(feat, half), v * BLOCK : (v + 1) * BLOCK] += rows

        @pl.when(brick >= own)
        def _():
            for v in range(VOX // BLOCK):
                rows = grads_ref[k, v * half : (v + 1) * half].astype(F32)
                mate_ref[brick - own, :, v * BLOCK : (v + 1) * BLOCK] += rows


def collect_halves(ids, grads, own, carried):
    amount, rows, _ = grads.shape
    half = FEAT // 2
    return pl.pallas_call(
        collect_halves_kernel,
        out_shape=(
            jax.ShapeDtypeStruct((own, FEAT, VOX), F32),
            jax.ShapeDtypeStruct((own, half, VOX), F32),
        ),
        grid_spec=pltpu.PrefetchScalarGridSpec(
            num_scalar_prefetch=1,
            grid=(amount // TAKE,),
            in_specs=[
                pl.BlockSpec((TAKE, rows, BLOCK), lambda i, ids: (i, 0, 0)),
                pl.BlockSpec(
                    (own, FEAT, VOX), lambda i, ids: (0, 0, 0), pipeline_mode=pl.Buffered(1)
                ),
            ],
            out_specs=(
                pl.BlockSpec((own, FEAT, VOX), lambda i, ids: (0, 0, 0)),
                pl.BlockSpec((own, half, VOX), lambda i, ids: (0, 0, 0)),
            ),
        ),
        compiler_params=pltpu.CompilerParams(vmem_limit_bytes=VMEM_LIMIT),
        cost_estimate=pl.CostEstimate(
            flops=amount * FEAT * VOX, bytes_accessed=amount * FEAT * VOX * 4, transcendentals=0
        ),
        name="collect_halves",
    )(ids, grads, carried)


MERGE = 16


def merge_kernel(core_ref, sums_ref, arrived_ref, out_ref):
    half = FEAT // 2
    feat = pl.multiple_of((1 - core_ref[0]) * half, half)
    out_ref[...] = sums_ref[...]
    out_ref[:, pl.ds(feat, half), :] += arrived_ref[...]


def merge(core, sums, arrived):
    own, half, _ = arrived.shape
    whole = pl.BlockSpec((MERGE, FEAT, VOX), lambda i, core: (i, 0, 0))
    return pl.pallas_call(
        merge_kernel,
        out_shape=jax.ShapeDtypeStruct(sums.shape, F32),
        grid_spec=pltpu.PrefetchScalarGridSpec(
            num_scalar_prefetch=1,
            grid=(own // MERGE,),
            in_specs=[whole, pl.BlockSpec((MERGE, half, VOX), lambda i, core: (i, 0, 0))],
            out_specs=whole,
        ),
        compiler_params=pltpu.CompilerParams(vmem_limit_bytes=VMEM_LIMIT),
        name="merge",
    )(core, sums, arrived)


def add_up_kernel(parts_ref, out_ref):
    parts = parts_ref[...].astype(F32)
    total = jnp.sum(parts[:, :8] + parts[:, 8:], axis=0, keepdims=True)
    out_ref[...] = jnp.broadcast_to(total, out_ref.shape)


def add_up(returned, rows):
    devices = returned.shape[0]
    return pl.pallas_call(
        add_up_kernel,
        out_shape=jax.ShapeDtypeStruct((devices, 8, BLOCK), F32),
        grid=(1,),
        in_specs=[pl.BlockSpec((devices, 16, BLOCK), lambda i: (0, rows // 16, 0))],
        out_specs=pl.BlockSpec((devices, 8, BLOCK), lambda i: (0, 0, 0)),
        name="add_up",
    )(returned)


def unpack_kernel(
    scale, totals_ref, w_in_ref, b_in_ref, w_hid_ref, b_hid_ref, w_out_ref, b_out_ref
):
    half = WIDTH // 2
    for side in range(2):
        lanes = slice(side * half, (side + 1) * half)
        w_hid_ref[:, lanes] = totals_ref[side * 256 : side * 256 + 256, :] * scale
        w_in_ref[:, lanes] = totals_ref[512 + side * 32 : 544 + side * 32, :] * scale
        w_out_ref[:, lanes] = totals_ref[576 + side * 8 : 580 + side * 8, :] * scale
        b_hid_ref[:, lanes] = totals_ref[592 + side * 8 : 593 + side * 8, :] * scale
        b_in_ref[:, lanes] = totals_ref[608 + side * 8 : 609 + side * 8, :] * scale
    for c in range(4):
        b_out_ref[c] = jnp.sum(totals_ref[624 + c : 625 + c, :]) * scale


def unpack(totals, scale):
    vmem = pl.BlockSpec(memory_space=pltpu.VMEM)
    shapes = ((FEAT, WIDTH), (1, WIDTH), (WIDTH, WIDTH), (1, WIDTH), (4, WIDTH), (4,))
    return pl.pallas_call(
        functools.partial(unpack_kernel, scale),
        out_shape=tuple(jax.ShapeDtypeStruct(shape, F32) for shape in shapes),
        in_specs=[vmem],
        out_specs=(vmem,) * 5 + (pl.BlockSpec(memory_space=pltpu.SMEM),),
        name="unpack",
    )(totals)


def exchange(values):
    return lax.all_to_all(values, AXES, split_axis=0, concat_axis=0, tiled=True)


def body(
    brick_feats,
    interp_weights,
    block_owner,
    block_brick,
    sample_count,
    target,
    w_in,
    b_in,
    w_hid,
    b_hid,
    w_out,
    b_out,
):
    own_blocks = interp_weights.shape[0]
    own_bricks = brick_feats.shape[0]
    dev_count = lax.axis_size(AXES)
    owners = block_owner[:, 0]
    space = lax.axis_size("space")
    me = lax.axis_index(AXES)
    core = lax.axis_index("view") % 2
    wish, lists = plan(owners, block_brick[:, 0], dev_count)
    wishes = exchange(jnp.broadcast_to(wish.reshape(1, 2, dev_count), (dev_count, 2, dev_count)))
    asked = [wishes[:, r, :] for r in range(2)]
    mine = [lax.dynamic_index_in_dim(a, me, axis=1, keepdims=False) for a in asked]
    other = me + (1 - 2 * core) * space
    others = lax.dynamic_index_in_dim(asked[1], other, axis=1, keepdims=False)
    others = jnp.where(others >= 0, others + own_bricks, -1)
    halves = jnp.where(mine[1] >= 0, mine[1], others)
    twice = (asked[1] >= 0).reshape(dev_count, dev_count // (2 * space), 2, space)
    crowded = jnp.any(twice[:, :, 0] & twice[:, :, 1])

    bricks_t = jnp.swapaxes(brick_feats, 1, 2)
    half = FEAT // 2
    swap = [(v, v ^ 1) for v in range(lax.axis_size("view"))]

    def part(which):
        return lax.dynamic_slice_in_dim(bricks_t, which * half, half, axis=1)

    chip_bricks = jnp.concatenate([part(core), lax.ppermute(part(1 - core), "view", swap)])
    fetched_0 = exchange(bricks_t[jnp.maximum(mine[0], 0)])
    sent_wholes = bricks_t[jnp.maximum(mine[1], 0)]
    sent_halves = chip_bricks[jnp.maximum(halves, 0)]
    sent_wholes, sent_halves = lax.optimization_barrier((sent_wholes, sent_halves))

    rays = jnp.concatenate([target, sample_count.astype(F32)[None]])
    rays = expand(rays.reshape(4, own_blocks, BLOCK // RAY_LEN))
    params = (w_in, b_in, w_hid, b_hid, w_out, b_out)
    nothing = jnp.zeros((8, BLOCK), F32)

    def rest(split, fetched_0, sent_1, ids_1, core, lists, owners, weights, rays, ids_0):
        stride = space if split else None
        rows = BLOCK // 2 if split else BLOCK
        fetched_1 = exchange(sent_1)
        grads_0, color_0, sums = run_blocks(
            True, lists, owners, weights, fetched_0, rays, params, nothing
        )
        grads_1, color_1, _ = run_blocks(
            False, lists, owners, weights, fetched_1, rays, params, sums, stride
        )
        returned_0 = exchange(grads_0)
        returned_1 = exchange(grads_1)
        partial = collect(ids_0, returned_0, own_bricks, None)
        totals = exchange(add_up(returned_1, rows))
        if split:
            grad, spare = collect_halves(
                jnp.concatenate([ids_1, core[None]]), returned_1, own_bricks, partial
            )
            grad = merge(core[None], grad, lax.ppermute(spare, "view", swap))
        else:
            grad = collect(ids_1, returned_1, own_bricks, partial)
        color = (color_0 + color_1)[:, :own_blocks, ::RAY_LEN].reshape(3, -1)
        return lax.optimization_barrier((grad, color, totals))

    common = (lists, owners, interp_weights, rays, mine[0])
    brick_grad, color, totals = lax.cond(
        crowded,
        lambda f, full, split, *c: rest(False, f, full, mine[1], core, *c),
        lambda f, full, split, *c: rest(True, f, split, halves, core, *c),
        fetched_0,
        sent_wholes,
        sent_halves,
        *common,
    )
    brick_grad = jnp.swapaxes(brick_grad, 1, 2)

    scale = 1.0 / (sample_count.shape[0] * dev_count)
    g_w_in, g_b_in, g_w_hid, g_b_hid, g_w_out, g_b_out = unpack(
        totals.reshape(GRAD_ROWS, BLOCK), scale
    )
    return (brick_grad, color, g_w_in, g_b_in[0], g_w_hid, g_b_hid[0], g_w_out, g_b_out)


def solution(mesh):
    shared = P(AXES, None, None)
    return jax.shard_map(
        body,
        mesh=mesh,
        in_specs=(
            shared,
            shared,
            P(AXES, None),
            P(AXES, None),
            P(AXES),
            P(None, AXES),
            P(),
            P(),
            P(),
            P(),
            P(),
            P(),
        ),
        out_specs=(shared, P(None, AXES), P(), P(), P(), P(), P(), P()),
        check_vma=False,
    )
```
